768 devices in a mesh: row: 24 (over z_lo, y), col: 32 (over z_hi, x, core).
Axes of the slice: x: 4, y: 8, z: 12 (z_hi: 4, z_lo: 3; z = z_hi * 3 + z_lo), core: 2. Of those that a mesh axis runs over, the one named last changes fastest.
Arguments:
- qkv: bfloat16 [9216, 3, 4096], P('row', None, 'col'), may hold values from -22 to 22
- out_weight: bfloat16 [4096, 8192], P(None, 'col'), may hold values from -0.09375 to 0.09375
- cotangent: bfloat16 [9216, 8192], P('row', 'col'), may hold values from -6 to 6
- scene_lengths: int32 [192], P('row'), may hold values from 8 to 328, as said below
- bucket_ids: int32 [192], P('row'), may hold values from 0 to 7
- sensor_ids: int32 [192], P('row'), may hold values from 0 to 7
- gsd_ids: int32 [192], P('row'), may hold values from 0 to 15
- step_ids: int32 [192], P('row'), may hold values from 0 to 999
- step_table: bfloat16 [1000, 8192], P(None, 'col'), may hold values from -3 to 3
- gsd_table: bfloat16 [16, 8192], P(None, 'col'), may hold values from -3 to 3
- sensor_table: bfloat16 [8, 8192], P(None, 'col'), may hold values from -3 to 3
- bucket_table: bfloat16 [8, 8192], P(None, 'col'), may hold values from -3 to 3
Outputs:
- mixed: bfloat16 [9216, 8192], P('row', 'col')
- grad_qkv: bfloat16 [9216, 3, 4096], P('row', None, 'col')
- grad_weight: bfloat16 [4096, 8192], P(None, 'col')
The draws below stay inside these ranges and needn't reach their ends.
Inputs may be any that keep to these rules, and one draw needn't show every extreme that they name: `scene_lengths`: each block of 384 tokens holds 8 scenes whose lengths are positive multiples of 8 and sum to 384.
All inputs are finite; a program needn't handle non-finite values.
Results may differ from the reference program's by a relative error of at most 0.03.
Values may be sent and summed in bfloat16 or wider, within the bound.
No kernel may reach another device: no remote copies, remote signals or barrier semaphores. Data moves between devices by JAX's collectives and lax.ppermute only.
A program may use at most 64 MiB of HBM per device.

```python
import jax
import jax.numpy as jnp
from jax import lax

D = 8192
HEADS = 32
HEAD = 128
TOK_ROW = 384
SCENES_ROW = 8
NT = 1000
NG = 16
NS = 8
NB = 8
HW = 4096
TOKENS = 9216
SCENES = 192
N_ROW = 24


def draw_qkv(key, part):
    base = jnp.clip(jax.random.normal(key, (TOKENS, 3, HW), jnp.float32), -4.0, 4.0)
    return base.astype(jnp.bfloat16)


def draw_scene_lengths(key, part):
    rows = SCENES // SCENES_ROW
    units = TOK_ROW // 8

    def one_row(row_key):
        cuts = jax.random.permutation(row_key, units - 1)[:SCENES_ROW - 1] + 1
        cuts = jnp.sort(cuts).astype(jnp.int32)
        edges = jnp.concatenate([jnp.zeros((1,), jnp.int32), cuts, jnp.full((1,), units, jnp.int32)])
        return (edges[1:] - edges[:-1]) * 8
    drawn = jax.vmap(one_row)(jax.random.split(key, rows))
    chosen_row = jax.random.randint(jax.random.fold_in(key, 101), (), 0, rows)
    chosen_place = jax.random.randint(jax.random.fold_in(key, 202), (), 0, SCENES_ROW)
    longest = TOK_ROW - 8 * (SCENES_ROW - 1)
    forced = jnp.where(jnp.arange(SCENES_ROW) == chosen_place, longest, 8).astype(jnp.int32)
    pick_row = (jnp.arange(rows) == chosen_row)[:, None]
    lengths = jnp.where(pick_row, forced[None, :], drawn)
    return lengths.reshape(-1).astype(jnp.int32)


def set_ends(values, key, low, high):
    shape = values.shape
    index_at = [jax.random.randint(jax.random.fold_in(key, axis), (), 0, shape[axis]) for axis in range(len(shape))]
    values = values.at[tuple(index_at)].set(low)
    longest = shape.index(max(shape))
    index_at[longest] = (index_at[longest] + 1) % shape[longest]
    return values.at[tuple(index_at)].set(high)


def shard_levels(rng, dims, cuts, low, high):
    def one(position, blocks):
        steps = jax.random.uniform(jax.random.fold_in(jax.random.fold_in(rng, 6), position), (blocks,), jnp.float32, low / len(cuts), high / len(cuts))
        return jnp.repeat(jnp.exp(steps), dims[position] // blocks).reshape((-1,) + (1,) * (len(dims) - position - 1))

    loudness = one(*cuts[0])
    for cut in cuts[1:]:
        loudness = loudness * one(*cut)
    return loudness


def normal_values(own_key, extent, deviation, limit, shards=(), kind=jnp.bfloat16):
    gain = shard_levels(own_key, extent, shards, -0.22, 0.18) if shards else 1.0
    values = jax.random.normal(own_key, extent, jnp.float32) * deviation * gain
    return jnp.minimum(jnp.maximum(values, -limit), limit).astype(kind)


def setup_inputs(seed: int = 0) -> dict:
    seeds = jax.random.split(jax.random.key(seed), 13)
    return {
        "qkv": draw_qkv(jax.random.fold_in(seeds[12], 71), 0),
        "out_weight": normal_values(seeds[1], (HW, D), HW ** -0.5, 0.09375, ((1, 32),)),
        "cotangent": normal_values(seeds[2], (TOKENS, D), 1.0, 6.0, ((0, 24), (1, 32))),
        "scene_lengths": draw_scene_lengths(jax.random.fold_in(seeds[12], 71), 0),
        "bucket_ids": set_ends(jax.random.randint(seeds[4], (SCENES,), 0, NB), jax.random.fold_in(seeds[4], 1), 0, NB - 1).astype(jnp.int32),
        "sensor_ids": set_ends(jax.random.randint(seeds[5], (SCENES,), 0, NS), jax.random.fold_in(seeds[5], 1), 0, NS - 1).astype(jnp.int32),
        "gsd_ids": set_ends(jax.random.randint(seeds[6], (SCENES,), 0, NG), jax.random.fold_in(seeds[6], 1), 0, NG - 1).astype(jnp.int32),
        "step_ids": set_ends(jax.random.randint(seeds[7], (SCENES,), 0, NT), jax.random.fold_in(seeds[7], 1), 0, NT - 1).astype(jnp.int32),
        "step_table": normal_values(seeds[8], (NT, D), 0.5, 3.0, ((1, 32),)),
        "gsd_table": normal_values(seeds[9], (NG, D), 0.5, 3.0, ((1, 32),)),
        "sensor_table": normal_values(seeds[10], (NS, D), 0.5, 3.0, ((1, 32),)),
        "bucket_table": normal_values(seeds[11], (NB, D), 0.5, 3.0, ((1, 32),)),
    }


def scene_of(lengths, count):
    ends = jnp.cumsum(lengths)
    places = jnp.arange(count)
    return jnp.sum((places[:, None] >= ends[None, :]).astype(jnp.int32), axis=1)


def lookup(ids, table):
    picks = (ids[:, None] == jnp.arange(table.shape[0])[None, :]).astype(table.dtype)
    return jnp.dot(picks, table, preferred_element_type=jnp.float32)


def attend(queries, keys, values, same):
    factor = HEAD ** -0.5
    scores = jnp.einsum("the,she->hts", queries.astype(jnp.float32), keys.astype(jnp.float32)) * factor
    scores = jnp.where(same[None], scores, -1e30)
    top = jnp.max(scores, axis=-1, keepdims=True)
    weights = jnp.exp(scores - top)
    probs = weights / jnp.sum(weights, axis=-1, keepdims=True)
    rounded = probs.astype(jnp.bfloat16)
    output = jnp.einsum("hts,she->the", rounded.astype(jnp.float32), values.astype(jnp.float32)).astype(jnp.bfloat16)
    return probs, rounded, output


def attend_back(queries, keys, values, probs, rounded, upstream):
    factor = HEAD ** -0.5
    upper = upstream.astype(jnp.float32)
    grad_values = jnp.einsum("hts,the->she", rounded.astype(jnp.float32), upper).astype(jnp.bfloat16)
    grad_probs = jnp.einsum("the,she->hts", upper, values.astype(jnp.float32))
    inner = jnp.sum(probs * grad_probs, axis=-1, keepdims=True)
    grad_scores = (probs * (grad_probs - inner)).astype(jnp.bfloat16).astype(jnp.float32)
    grad_queries = (jnp.einsum("hts,she->the", grad_scores, keys.astype(jnp.float32)) * factor).astype(jnp.bfloat16)
    grad_keys = (jnp.einsum("hts,the->she", grad_scores, queries.astype(jnp.float32)) * factor).astype(jnp.bfloat16)
    stacked = jnp.stack([grad_queries, grad_keys, grad_values], axis=1)
    return stacked.reshape(stacked.shape[0], 3, stacked.shape[2] * stacked.shape[3])


def reference(qkv, out_weight, cotangent, scene_lengths, bucket_ids, sensor_ids, gsd_ids, step_ids, step_table, gsd_table, sensor_table, bucket_table):
    gate_scene = lookup(step_ids, step_table) + lookup(gsd_ids, gsd_table)
    gate_scene = gate_scene + lookup(sensor_ids, sensor_table) + lookup(bucket_ids, bucket_table)
    lengths_rows = scene_lengths.reshape(N_ROW, SCENES_ROW)
    segments = jax.vmap(lambda lengths: scene_of(lengths, TOK_ROW))(lengths_rows)
    global_scene = segments + SCENES_ROW * jnp.arange(N_ROW, dtype=jnp.int32)[:, None]
    gate = gate_scene[global_scene.reshape(-1)]
    blocks = qkv.reshape(N_ROW, TOK_ROW, 3, HEADS, HEAD)

    def forward_row(items):
        block, segs = items
        same = segs[:, None] == segs[None, :]
        probs, rounded, output = attend(block[:, 0], block[:, 1], block[:, 2], same)
        return output.reshape(TOK_ROW, HW)

    attended = lax.map(forward_row, (blocks, segments)).reshape(TOKENS, HW)
    projected = jnp.dot(attended, out_weight, preferred_element_type=jnp.float32)
    mixed = (gate * projected).astype(jnp.bfloat16)
    gated = (gate * cotangent.astype(jnp.float32)).astype(jnp.bfloat16)
    upstream = jnp.dot(gated, out_weight.T, preferred_element_type=jnp.float32).astype(jnp.bfloat16)
    upstream_rows = upstream.reshape(N_ROW, TOK_ROW, HEADS, HEAD)

    def backward_row(items):
        block, segs, upper = items
        same = segs[:, None] == segs[None, :]
        probs, rounded, output = attend(block[:, 0], block[:, 1], block[:, 2], same)
        return attend_back(block[:, 0], block[:, 1], block[:, 2], probs, rounded, upper)

    grad_qkv = lax.map(backward_row, (blocks, segments, upstream_rows)).reshape(TOKENS, 3, HW)

    def add_row(total, items):
        attended_row, gated_row = items
        partial_sum = jnp.dot(attended_row.T, gated_row, preferred_element_type=jnp.float32).astype(jnp.bfloat16)
        partial_sum = lax.optimization_barrier(partial_sum)
        return total + partial_sum.astype(jnp.float32), None

    total, unused = lax.scan(add_row, jnp.zeros((HW, D), jnp.float32), (attended.reshape(N_ROW, TOK_ROW, HW), gated.reshape(N_ROW, TOK_ROW, D)))
    return mixed, grad_qkv, total.astype(jnp.bfloat16)
```

```python
import jax
import jax.numpy as jnp
from jax import lax
from jax.sharding import Mesh, PartitionSpec as P

HEAD = 128
ROW = ("zlo", "y")
COL = ("zhi", "x", "core")
F32 = jnp.float32
BF = jnp.bfloat16


def scene_of(lengths, count):
    ends = jnp.cumsum(lengths)
    places = jnp.arange(count)
    return jnp.sum((places[:, None] >= ends[None, :]).astype(jnp.int32), axis=1)


def lookup(ids, table):
    picks = (ids[:, None] == jnp.arange(table.shape[0])[None, :]).astype(table.dtype)
    return jnp.dot(picks, table, preferred_element_type=F32)


def dot(a, b, dims):
    return lax.dot_general(a, b, (dims, ((), ())), preferred_element_type=F32)


def shift(value, axis, size, step):
    return lax.ppermute(value, axis, [(i, (i + step) % size) for i in range(size)])


def on_device(
    qkv,
    out_weight,
    cotangent,
    scene_lengths,
    bucket_ids,
    sensor_ids,
    gsd_ids,
    step_ids,
    step_table,
    gsd_table,
    sensor_table,
    bucket_table,
):
    toks = qkv.shape[0]
    width = cotangent.shape[1]
    factor = HEAD ** (-0.5)
    n_core, n_x, n_zhi = lax.axis_size("core"), lax.axis_size("x"), lax.axis_size("zhi")
    n_y, n_zlo = lax.axis_size("y"), lax.axis_size("zlo")
    core, x = lax.axis_index("core"), lax.axis_index("x")

    segments = scene_of(scene_lengths, toks)
    same = segments[:, None] == segments[None, :]
    queries, keys, values = qkv[:, 0], qkv[:, 1], qkv[:, 2]

    scores = dot(queries, keys, ((1,), (1,))) * factor
    scores = jnp.where(same, scores, -1e30)
    top = jnp.max(scores, axis=-1, keepdims=True)
    weights = jnp.exp(scores - top)
    probs = weights / jnp.sum(weights, axis=-1, keepdims=True)
    rounded = probs.astype(BF)
    attended = dot(values, rounded, ((0,), (1,))).astype(BF)

    gathered = lax.all_gather(attended, "zhi", axis=0, tiled=True)

    gate_scene = lookup(step_ids, step_table) + lookup(gsd_ids, gsd_table)
    gate_scene = gate_scene + lookup(sensor_ids, sensor_table) + lookup(bucket_ids, bucket_table)
    member = (segments[:, None] == jnp.arange(scene_lengths.shape[0])[None, :]).astype(F32)
    gate = jnp.dot(member, gate_scene, precision=lax.Precision.HIGHEST, preferred_element_type=F32)
    gated = (gate * cotangent.astype(F32)).astype(BF)

    weight = out_weight.reshape(n_zhi, n_x, n_core, HEAD, width)
    weight = weight.transpose(2, 1, 0, 3, 4).reshape(n_core, n_x * n_zhi * HEAD, width)

    theirs = lax.dynamic_index_in_dim(weight, 1 - core, 0, keepdims=False)
    mine = lax.dynamic_index_in_dim(weight, core, 0, keepdims=False)
    sent = dot(theirs, gated, ((1,), (1,))).astype(BF)
    got = shift(sent, "core", n_core, 1)
    summed = (dot(mine, gated, ((1,), (1,))) + got.astype(F32)).astype(BF)
    summed = lax.psum_scatter(summed, "x", scatter_dimension=0, tiled=True)
    summed = lax.psum_scatter(summed, "zhi", scatter_dimension=0, tiled=True)

    pieces = [gathered] + [shift(gathered, "x", n_x, s) for s in range(1, n_x)]
    stacked = jnp.stack(pieces)
    order = jnp.mod(x - jnp.arange(n_x), n_x)
    del order
    ring = jnp.concatenate([stacked, stacked])
    ring = jnp.flip(ring, 0)
    ring = lax.dynamic_slice_in_dim(ring, n_x - 1 - x, n_x, 0)
    half = ring.reshape(n_x * n_zhi * HEAD, toks)
    other = shift(half, "core", n_core, 1)
    first = jnp.where(core == 0, half, other)
    second = jnp.where(core == 0, other, half)
    heads = jnp.concatenate([first, second])

    partial_sum = dot(heads, gated, ((1,), (0,))).astype(BF)
    spread = lax.all_to_all(partial_sum, "y", split_axis=0, concat_axis=0, tiled=True)
    spread = spread.reshape(n_y, -1, width).astype(F32).sum(0).astype(BF)
    total = spread.astype(F32)
    for s in range(1, n_zlo):
        total = total + shift(spread, "zlo", n_zlo, s).astype(F32)
    total = lax.all_gather(total.astype(BF), "y", axis=0, tiled=True)
    total = total.reshape(n_core, n_x, n_zhi, HEAD, width).transpose(2, 1, 0, 3, 4)
    total = total.reshape(-1, width)

    projected = dot(heads, weight.reshape(-1, width), ((0,), (0,)))
    mixed = (gate * projected).astype(BF)

    upstream = summed.T
    grad_values = dot(rounded, upstream, ((0,), (0,))).astype(BF)
    grad_probs = dot(upstream, values, ((1,), (1,)))
    inner = jnp.sum(probs * grad_probs, axis=-1, keepdims=True)
    grad_scores = (probs * (grad_probs - inner)).astype(BF)
    grad_queries = (dot(grad_scores, keys, ((1,), (0,))) * factor).astype(BF)
    grad_keys = (dot(grad_scores, queries, ((0,), (0,))) * factor).astype(BF)
    grad_qkv = jnp.stack([grad_queries, grad_keys, grad_values], axis=1)
    return (mixed, grad_qkv, total)


def solution(mesh):
    fine = Mesh(mesh.devices.reshape(3, 8, 4, 4, 2), ROW + COL)
    return jax.shard_map(
        on_device,
        mesh=fine,
        in_specs=(
            P(ROW, None, COL),
            P(None, COL),
            P(ROW, COL),
            P(ROW),
            P(ROW),
            P(ROW),
            P(ROW),
            P(ROW),
            P(None, COL),
            P(None, COL),
            P(None, COL),
            P(None, COL),
        ),
        out_specs=(P(ROW, COL), P(ROW, None, COL), P(None, COL)),
        check_vma=False,
    )
```

```python
import jax
import jax.numpy as jnp
from jax import lax
from jax.experimental import pallas as pl
from jax.experimental.pallas import tpu as pltpu
from jax.sharding import Mesh, PartitionSpec as P

HEAD = 128
ROW = ("zlo", "y")
COL = ("zhi", "x", "core")
NZLO, NY, NZHI, NX, NCORE = 3, 8, 4, 4, 2
F32 = jnp.float32
BF = jnp.bfloat16
LIMIT = 32 * 1024 * 1024
SMEM = pl.BlockSpec(memory_space=pltpu.SMEM)
VMEM = pl.BlockSpec(memory_space=pltpu.VMEM)
ANY = pl.BlockSpec(memory_space=pl.ANY)


def scene_of(lengths, count):
    ends = jnp.cumsum(lengths)
    places = jnp.arange(count)
    return jnp.sum((places[:, None] >= ends[None, :]).astype(jnp.int32), axis=1)


def lookup(ids, table):
    picks = (ids[:, None] == jnp.arange(table.shape[0])[None, :]).astype(table.dtype)
    return jnp.dot(picks, table, preferred_element_type=F32)


def dot(a, b, dims):
    return lax.dot_general(a, b, (dims, ((), ())), preferred_element_type=F32)


def shift(value, axis, size, step):
    return lax.ppermute(value, axis, [(i, (i + step) % size) for i in range(size)])


def after(value, *others):
    return lax.optimization_barrier((value,) + others)[0]


def call(body, out_shape, in_specs, out_specs, flops, nbytes, scratch=()):
    return pl.pallas_call(
        body,
        out_shape=out_shape,
        in_specs=in_specs,
        out_specs=out_specs,
        scratch_shapes=list(scratch),
        compiler_params=pltpu.CompilerParams(vmem_limit_bytes=LIMIT),
        cost_estimate=pl.CostEstimate(flops=flops, bytes_accessed=nbytes, transcendentals=0),
    )


def up_body(place, weight, gated, *refs):
    out = refs[-1]
    core = place[1]
    pick = core if len(refs) == 2 else 1 - core
    for x in range(NX):
        for z in range(NZHI):
            rows = pl.ds((x * NZHI + z) * HEAD, HEAD)
            value = dot(weight[(z * NX + x) * NCORE + pick], gated[...], ((1,), (1,)))
            if len(refs) == 2:
                value = value + refs[0][rows, :].astype(F32)
            out[rows, :] = value.astype(BF)


def upstream_part(place, weight, gated, *got):
    toks = gated.shape[0]
    rows = NX * NZHI * HEAD
    return call(
        up_body,
        jax.ShapeDtypeStruct((rows, toks), BF),
        [SMEM] + [VMEM] * (2 + len(got)),
        VMEM,
        2 * rows * toks * gated.shape[1],
        4 * rows * toks,
    )(place, weight, gated, *got)


def part_body(*refs):
    *pieces, gated, out = refs
    rows = pieces[0].shape[0]
    for i, piece in enumerate(pieces):
        out[i * rows : (i + 1) * rows, :] = dot(piece[...], gated[...], ((1,), (0,))).astype(BF)


def weight_part(pieces, gated):
    rows = sum(p.shape[0] for p in pieces)
    toks, width = gated.shape
    return call(
        part_body,
        jax.ShapeDtypeStruct((rows, width), BF),
        [VMEM] * (len(pieces) + 1),
        VMEM,
        2 * rows * toks * width,
        2 * rows * (toks + width),
    )(*pieces, gated)


def mix_body(place, weight, gate, *refs):
    *pieces, out, acc = refs
    x, core = place[0], place[1]
    for i, piece in enumerate(pieces):
        s, c = i // 2, i % 2
        chip = lax.rem(x + NX - s, NX)
        pick = core if c == 0 else 1 - core
        rows = jnp.concatenate([weight[(z * NX + chip) * NCORE + pick] for z in range(NZHI)])
        value = dot(piece[...], rows, ((0,), (0,)))
        acc[...] = value if i == 0 else acc[...] + value
    out[...] = (gate[...] * acc[...]).astype(BF)


def mix(place, weight, gate, pieces):
    toks, width = gate.shape
    rows = sum(p.shape[0] for p in pieces)
    return call(
        mix_body,
        jax.ShapeDtypeStruct((toks, width), BF),
        [SMEM] + [VMEM] * (2 + len(pieces)),
        VMEM,
        2 * rows * toks * width,
        2 * rows * (toks + width),
        [pltpu.VMEM((toks, width), F32)],
    )(place, weight, gate, *pieces)


def place_body(place, src, dst, sems):
    x, core = place[0], place[1]
    copies = []
    for y in range(NY):
        for b in range(4):
            if b == 0:
                i, s = y, 0
            else:
                i = 3 * y + b - 1
                s, i = 1 + i // 8, i % 8
            c, z = i // NZHI, i % NZHI
            chip = lax.rem(x + NX - s, NX)
            head = (z * NX + chip) * NCORE + (core if c == 0 else 1 - core)
            copies.append(pltpu.make_async_copy(src.at[y * 4 + b], dst.at[head], sems.at[y * 4 + b]))
    for copy in copies:
        copy.start()
    for copy in copies:
        copy.wait()


def put_heads(place, total):
    heads = total.shape[0] // HEAD
    return call(
        place_body,
        jax.ShapeDtypeStruct((heads, HEAD, total.shape[1]), BF),
        [SMEM, ANY],
        ANY,
        0,
        4 * total.size,
        [pltpu.SemaphoreType.DMA((heads,))],
    )(place, total.reshape(heads, HEAD, -1)).reshape(total.shape)


def exchange(part):
    spread = lax.all_to_all(part, "y", split_axis=0, concat_axis=0, tiled=True)
    return spread


def fold(spread):
    return spread.reshape(NY, -1, spread.shape[1]).astype(F32).sum(0).astype(BF)


def fold_zlo(value):
    total = value.astype(F32)
    for s in range(1, NZLO):
        total = total + shift(value, "zlo", NZLO, s).astype(F32)
    return total.astype(BF)


def on_device(
    qkv,
    out_weight,
    cotangent,
    scene_lengths,
    bucket_ids,
    sensor_ids,
    gsd_ids,
    step_ids,
    step_table,
    gsd_table,
    sensor_table,
    bucket_table,
):
    toks = qkv.shape[0]
    width = cotangent.shape[1]
    factor = HEAD ** (-0.5)
    place = jnp.stack([lax.axis_index("x"), lax.axis_index("core")]).astype(jnp.int32)
    weight = out_weight.reshape(-1, HEAD, width)

    segments = scene_of(scene_lengths, toks)
    same = segments[:, None] == segments[None, :]
    queries, keys, values = qkv[:, 0], qkv[:, 1], qkv[:, 2]

    scores = dot(queries, keys, ((1,), (1,))) * factor
    scores = jnp.where(same, scores, -1e30)
    top = jnp.max(scores, axis=-1, keepdims=True)
    weights = jnp.exp(scores - top)
    probs = weights / jnp.sum(weights, axis=-1, keepdims=True)
    rounded = probs.astype(BF)
    attended = dot(values, rounded, ((0,), (1,))).astype(BF)

    gate_scene = lookup(step_ids, step_table) + lookup(gsd_ids, gsd_table)
    gate_scene = gate_scene + lookup(sensor_ids, sensor_table) + lookup(bucket_ids, bucket_table)
    member = (segments[:, None] == jnp.arange(scene_lengths.shape[0])[None, :]).astype(F32)
    gate = jnp.dot(member, gate_scene, precision=lax.Precision.HIGHEST, preferred_element_type=F32)
    gated = (gate * cotangent.astype(F32)).astype(BF)

    own = {0: lax.all_gather(attended, "zhi", axis=0, tiled=True)}
    for s in (1, 3, 2):
        own[s] = shift(own[0], "x", NX, s)

    sent = upstream_part(place, weight, gated)
    got = shift(sent, "core", NCORE, 1)
    summed = upstream_part(place, weight, gated, got)

    other = {0: shift(own[0], "core", NCORE, 1)}
    first = weight_part([own[0], other[0]], gated)
    first = exchange(first)

    held = lax.optimization_barrier((own[1], own[2], own[3], summed))
    own[1], own[2], own[3], summed = held
    summed = lax.psum_scatter(summed, "x", scatter_dimension=0, tiled=True)
    summed = lax.psum_scatter(summed, "zhi", scatter_dimension=0, tiled=True)

    for s in (1, 3, 2):
        other[s] = shift(own[s], "core", NCORE, 1)
    second = weight_part([p for s in (1, 2, 3) for p in (own[s], other[s])], gated)
    second = exchange(second)
    first = fold_zlo(fold(first))
    second = fold_zlo(fold(second))
    total = jnp.concatenate([first, second])
    total = lax.all_gather(total, "y", axis=0, tiled=True)
    total = put_heads(place, total)

    mixed = mix(place, weight, gate, [p for s in range(NX) for p in (own[s], other[s])])

    upstream = summed.T
    grad_values = dot(rounded, upstream, ((0,), (0,))).astype(BF)
    grad_probs = dot(upstream, values, ((1,), (1,)))
    inner = jnp.sum(probs * grad_probs, axis=-1, keepdims=True)
    grad_scores = (probs * (grad_probs - inner)).astype(BF)
    grad_queries = (dot(grad_scores, keys, ((1,), (0,))) * factor).astype(BF)
    grad_keys = (dot(grad_scores, queries, ((0,), (0,))) * factor).astype(BF)
    grad_qkv = jnp.stack([grad_queries, grad_keys, grad_values], axis=1)
    return (mixed, grad_qkv, total)


def solution(mesh):
    fine = Mesh(mesh.devices.reshape(NZLO, NY, NZHI, NX, NCORE), ROW + COL)
    return jax.shard_map(
        on_device,
        mesh=fine,
        in_specs=(
            P(ROW, None, COL),
            P(None, COL),
            P(ROW, COL),
            P(ROW),
            P(ROW),
            P(ROW),
            P(ROW),
            P(ROW),
            P(None, COL),
            P(None, COL),
            P(None, COL),
            P(None, COL),
        ),
        out_specs=(P(ROW, COL), P(ROW, None, COL), P(None, COL)),
        check_vma=False,
    )
```

```python
import jax
import jax.numpy as jnp
from jax import lax
from jax.experimental import pallas as pl
from jax.experimental.pallas import tpu as pltpu
from jax.sharding import Mesh, PartitionSpec as P

HEAD = 128
ROW = ("zlo", "y")
COL = ("zhi", "x", "core")
NZLO, NY, NZHI, NX, NCORE = 3, 8, 4, 4, 2
SLAB = HEAD // NY
F32 = jnp.float32
BF = jnp.bfloat16
SMEM = pl.BlockSpec(memory_space=pltpu.SMEM)
VMEM = pl.BlockSpec(memory_space=pltpu.VMEM)
HBM = pl.BlockSpec(memory_space=pltpu.HBM)


def scene_of(lengths, count):
    ends = jnp.cumsum(lengths)
    places = jnp.arange(count)
    return jnp.sum((places[:, None] >= ends[None, :]).astype(jnp.int32), axis=1)


def lookup(ids, table):
    picks = (ids[:, None] == jnp.arange(table.shape[0])[None, :]).astype(table.dtype)
    return jnp.dot(picks, table, preferred_element_type=F32)


def dot(a, b, dims):
    return lax.dot_general(a, b, (dims, ((), ())), preferred_element_type=F32)


def shift(value, axis, size, step):
    return lax.ppermute(value, axis, [(i, (i + step) % size) for i in range(size)])


def after(value, *others):
    return lax.optimization_barrier((value,) + others)[0]


def call(body, out_shape, in_specs, out_specs, flops, nbytes, scratch=(), limit=60):
    return pl.pallas_call(
        body,
        out_shape=out_shape,
        in_specs=in_specs,
        out_specs=out_specs,
        scratch_shapes=list(scratch),
        compiler_params=pltpu.CompilerParams(vmem_limit_bytes=limit * 1024 * 1024),
        cost_estimate=pl.CostEstimate(flops=flops, bytes_accessed=nbytes, transcendentals=0),
    )


def up_body(place, weight, gated, *refs):
    out = refs[-1]
    core = place[1]
    pick = core if len(refs) == 2 else 1 - core
    for x in range(NX):
        for z in range(NZHI):
            rows = pl.ds((x * NZHI + z) * HEAD, HEAD)
            value = dot(weight[(z * NX + x) * NCORE + pick], gated[...], ((1,), (1,)))
            if len(refs) == 2:
                value = value + refs[0][rows, :].astype(F32)
            out[rows, :] = value.astype(BF)


def upstream_part(place, weight, gated, *got):
    toks = gated.shape[0]
    rows = NX * NZHI * HEAD
    return call(
        up_body,
        jax.ShapeDtypeStruct((rows, toks), BF),
        [SMEM] + [VMEM] * (2 + len(got)),
        VMEM,
        2 * rows * toks * gated.shape[1],
        4 * rows * toks,
        limit=16,
    )(place, weight, gated, *got)


def fetch(pieces, held, sems):
    copies = [pltpu.make_async_copy(p, held.at[i], sems.at[i]) for i, p in enumerate(pieces)]
    for copy in copies:
        copy.start()
    for copy in copies:
        copy.wait()


def fetch_scratch(pieces):
    count = len(pieces)
    return [pltpu.VMEM((count, *pieces[0].shape), BF), pltpu.SemaphoreType.DMA((count,))]


def slabs(held, y):
    starts = [z * HEAD + y * SLAB for z in range(NZHI)]
    return jnp.concatenate(
        [held[i, start : start + SLAB, :] for i in range(held.shape[0]) for start in starts]
    )


def part_body(*refs):
    *pieces, gated, out, acc, held, sems = refs
    fetch(pieces, held, sems)
    toks = held.shape[2]
    for y in range(NY):
        value = dot(slabs(held, y), gated[y * toks : (y + 1) * toks, :], ((1,), (0,)))
        acc[...] = value if y == 0 else acc[...] + value
    out[...] = acc[...].astype(BF)


def weight_part(pieces, gated):
    rows = sum(p.shape[0] for p in pieces) // NY
    toks, width = gated.shape
    return call(
        part_body,
        jax.ShapeDtypeStruct((rows, width), BF),
        [HBM] * len(pieces) + [VMEM],
        VMEM,
        2 * rows * toks * width,
        2 * rows * (toks + width),
        [pltpu.VMEM((rows, width), F32)] + fetch_scratch(pieces),
    )(*pieces, gated)


def mix_body(place, weight, *refs):
    *pieces, out, held, sems = refs
    fetch(pieces, held, sems)
    x, core, mine = place[0], place[1], place[2]
    rows = []
    for i in range(len(pieces)):
        s, c = i // 2, i % 2
        chip = lax.rem(x + NX - s, NX)
        pick = core if c == 0 else 1 - core
        for z in range(NZHI):
            start = pl.multiple_of(mine * SLAB, SLAB)
            rows.append(weight[(z * NX + chip) * NCORE + pick, pl.ds(start, SLAB), :])
    rows = jnp.concatenate(rows)
    for y in range(NY):
        out[y] = dot(slabs(held, y), rows, ((0,), (0,))).astype(BF)


def mix_part(place, weight, pieces):
    toks, width = pieces[0].shape[1], weight.shape[2]
    rows = sum(p.shape[0] for p in pieces)
    return call(
        mix_body,
        jax.ShapeDtypeStruct((NY, toks, width), BF),
        [SMEM, VMEM] + [HBM] * len(pieces),
        VMEM,
        2 * rows * toks * width,
        2 * rows * (toks + width),
        fetch_scratch(pieces),
    )(place, weight, *pieces)


def place_body(place, src, dst, sems):
    x, core = place[0], place[1]
    copies = []
    for i in range(NX * NCORE * NZHI):
        s, c, z = i // (NCORE * NZHI), i // NZHI % NCORE, i % NZHI
        chip = lax.rem(x + NX - s, NX)
        head = (z * NX + chip) * NCORE + (core if c == 0 else 1 - core)
        copies.append(pltpu.make_async_copy(src.at[:, i], dst.at[head], sems.at[i]))
    for copy in copies:
        copy.start()
    for copy in copies:
        copy.wait()


def put_heads(place, total):
    heads, width = NX * NCORE * NZHI, total.shape[1]
    return call(
        place_body,
        jax.ShapeDtypeStruct((heads, NY, SLAB, width), BF),
        [SMEM, HBM],
        HBM,
        0,
        4 * total.size,
        [pltpu.SemaphoreType.DMA((heads,))],
    )(place, total.reshape(NY, heads, SLAB, width)).reshape(total.shape)


def fold_zlo(value):
    total = value.astype(F32)
    for s in range(1, NZLO):
        total = total + shift(value, "zlo", NZLO, s).astype(F32)
    return total.astype(BF)


def on_device(
    qkv,
    out_weight,
    cotangent,
    scene_lengths,
    bucket_ids,
    sensor_ids,
    gsd_ids,
    step_ids,
    step_table,
    gsd_table,
    sensor_table,
    bucket_table,
):
    toks = qkv.shape[0]
    width = cotangent.shape[1]
    factor = HEAD ** (-0.5)
    place = jnp.stack([lax.axis_index(a) for a in ("x", "core", "y")]).astype(jnp.int32)
    weight = out_weight.reshape(-1, HEAD, width)

    segments = scene_of(scene_lengths, toks)
    same = segments[:, None] == segments[None, :]
    queries, keys, values = qkv[:, 0], qkv[:, 1], qkv[:, 2]

    scores = dot(queries, keys, ((1,), (1,))) * factor
    scores = jnp.where(same, scores, -1e30)
    top = jnp.max(scores, axis=-1, keepdims=True)
    weights = jnp.exp(scores - top)
    probs = weights / jnp.sum(weights, axis=-1, keepdims=True)
    rounded = probs.astype(BF)
    attended = dot(values, rounded, ((0,), (1,))).astype(BF)

    gate_scene = lookup(step_ids, step_table) + lookup(gsd_ids, gsd_table)
    gate_scene = gate_scene + lookup(sensor_ids, sensor_table) + lookup(bucket_ids, bucket_table)
    member = (segments[:, None] == jnp.arange(scene_lengths.shape[0])[None, :]).astype(F32)
    gate = jnp.dot(member, gate_scene, precision=lax.Precision.HIGHEST, preferred_element_type=F32)
    gated = (gate * cotangent.astype(F32)).astype(BF)

    gated_y = lax.all_gather(gated, "y", axis=0, tiled=True)

    sent = upstream_part(place, weight, gated)
    got = shift(sent, "core", NCORE, 1)

    attended, sent = lax.optimization_barrier((attended, sent))
    attended = lax.all_to_all(attended, "y", split_axis=0, concat_axis=0, tiled=True)

    summed = upstream_part(place, weight, gated, got)
    attended, summed = lax.optimization_barrier((attended, summed))
    summed = lax.psum_scatter(summed, "x", scatter_dimension=0, tiled=True)

    own = {0: lax.all_gather(attended, "zhi", axis=0, tiled=True)}
    for s in (1, 3, 2):
        own[s] = shift(own[0], "x", NX, s)
    pieces = [p for s in range(NX) for p in (own[s], shift(own[s], "core", NCORE, 1))]

    total = weight_part(pieces, gated_y)
    *pieces, total, summed = lax.optimization_barrier((*pieces, total, summed))
    parts = mix_part(place, weight, pieces)
    total, parts = lax.optimization_barrier((fold_zlo(total), parts))
    total = lax.all_gather(total, "y", axis=0, tiled=True)
    total = put_heads(place, total)

    summed = lax.psum_scatter(summed, "zhi", scatter_dimension=0, tiled=True)

    parts = lax.all_to_all(parts, "y", split_axis=0, concat_axis=0, tiled=True)
    mixed = (gate * parts.astype(F32).sum(0)).astype(BF)

    upstream = summed.T
    grad_values = dot(rounded, upstream, ((0,), (0,))).astype(BF)
    grad_probs = dot(upstream, values, ((1,), (1,)))
    inner = jnp.sum(probs * grad_probs, axis=-1, keepdims=True)
    grad_scores = (probs * (grad_probs - inner)).astype(BF)
    grad_queries = (dot(grad_scores, keys, ((1,), (0,))) * factor).astype(BF)
    grad_keys = (dot(grad_scores, queries, ((0,), (0,))) * factor).astype(BF)
    grad_qkv = jnp.stack([grad_queries, grad_keys, grad_values], axis=1)
    return (mixed, grad_qkv, total)


def solution(mesh):
    fine = Mesh(mesh.devices.reshape(NZLO, NY, NZHI, NX, NCORE), ROW + COL)
    return jax.shard_map(
        on_device,
        mesh=fine,
        in_specs=(
            P(ROW, None, COL),
            P(None, COL),
            P(ROW, COL),
            P(ROW),
            P(ROW),
            P(ROW),
            P(ROW),
            P(ROW),
            P(None, COL),
            P(None, COL),
            P(None, COL),
            P(None, COL),
        ),
        out_specs=(P(ROW, COL), P(ROW, None, COL), P(None, COL)),
        check_vma=False,
    )
```

```python
import jax
import jax.numpy as jnp
from jax import lax
from jax.experimental import pallas as pl
from jax.experimental.pallas import tpu as pltpu
from jax.sharding import Mesh, PartitionSpec as P

HEAD = 128
ROW = ("zlo", "y")
COL = ("zhi", "x", "core")
NZLO, NY, NZHI, NX, NCORE = 3, 8, 4, 4, 2
SLAB = HEAD // NY
F32 = jnp.float32
BF = jnp.bfloat16
SMEM = pl.BlockSpec(memory_space=pltpu.SMEM)
VMEM = pl.BlockSpec(memory_space=pltpu.VMEM)
HBM = pl.BlockSpec(memory_space=pltpu.HBM)


def scene_of(lengths, count):
    ends = jnp.cumsum(lengths)
    places = jnp.arange(count)
    return jnp.sum((places[:, None] >= ends[None, :]).astype(jnp.int32), axis=1)


def lookup(ids, table):
    picks = (ids[:, None] == jnp.arange(table.shape[0])[None, :]).astype(table.dtype)
    return jnp.dot(picks, table, preferred_element_type=F32)


def dot(a, b, dims):
    return lax.dot_general(a, b, (dims, ((), ())), preferred_element_type=F32)


def shift(value, axis, size, step):
    return lax.ppermute(value, axis, [(i, (i + step) % size) for i in range(size)])


def after(value, *others):
    return lax.optimization_barrier((value,) + others)[0]


def call(body, out_shape, in_specs, out_specs, flops, nbytes, scratch=(), limit=60):
    return pl.pallas_call(
        body,
        out_shape=out_shape,
        in_specs=in_specs,
        out_specs=out_specs,
        scratch_shapes=list(scratch),
        compiler_params=pltpu.CompilerParams(vmem_limit_bytes=limit * 1024 * 1024),
        cost_estimate=pl.CostEstimate(flops=flops, bytes_accessed=nbytes, transcendentals=0),
    )


def up_body(place, weight, gated, *refs):
    out = refs[-1]
    core = place[1]
    pick = core if len(refs) == 2 else 1 - core
    for x in range(NX):
        for z in range(NZHI):
            rows = pl.ds((x * NZHI + z) * HEAD, HEAD)
            value = dot(weight[(z * NX + x) * NCORE + pick], gated[...], ((1,), (1,)))
            if len(refs) == 2:
                value = value + refs[0][rows, :].astype(F32)
            out[rows, :] = value.astype(BF)


def upstream_part(place, weight, gated, *got):
    toks = gated.shape[0]
    rows = NX * NZHI * HEAD
    return call(
        up_body,
        jax.ShapeDtypeStruct((rows, toks), BF),
        [SMEM] + [VMEM] * (2 + len(got)),
        VMEM,
        2 * rows * toks * gated.shape[1],
        4 * rows * toks,
        limit=16,
    )(place, weight, gated, *got)


def fetch(pieces, held, sems):
    copies = [pltpu.make_async_copy(p, held.at[i], sems.at[i]) for i, p in enumerate(pieces)]
    for copy in copies:
        copy.start()
    for copy in copies:
        copy.wait()


def fetch_scratch(pieces):
    count = len(pieces)
    return [pltpu.VMEM((count, *pieces[0].shape), BF), pltpu.SemaphoreType.DMA((count,))]


def slabs(held, y):
    starts = [z * HEAD + y * SLAB for z in range(NZHI)]
    return jnp.concatenate(
        [held[i, start : start + SLAB, :] for i in range(held.shape[0]) for start in starts]
    )


def part_body(*refs):
    *pieces, gated, out, acc, held, sems = refs
    fetch(pieces, held, sems)
    toks = held.shape[2]
    for y in range(NY):
        value = dot(slabs(held, y), gated[y * toks : (y + 1) * toks, :], ((1,), (0,)))
        acc[...] = value if y == 0 else acc[...] + value
    out[...] = acc[...].astype(BF)


def weight_part(pieces, gated):
    rows = sum(p.shape[0] for p in pieces) // NY
    toks, width = gated.shape
    return call(
        part_body,
        jax.ShapeDtypeStruct((rows, width), BF),
        [HBM] * len(pieces) + [VMEM],
        VMEM,
        2 * rows * toks * width,
        2 * rows * (toks + width),
        [pltpu.VMEM((rows, width), F32)] + fetch_scratch(pieces),
    )(*pieces, gated)


def mix_body(place, weight, *refs):
    *pieces, out, held, sems = refs
    fetch(pieces, held, sems)
    x, core, mine = place[0], place[1], place[2]
    rows = []
    for i in range(len(pieces)):
        s, c = i // 2, i % 2
        chip = lax.rem(x + NX - s, NX)
        pick = core if c == 0 else 1 - core
        for z in range(NZHI):
            start = pl.multiple_of(mine * SLAB, SLAB)
            rows.append(weight[(z * NX + chip) * NCORE + pick, pl.ds(start, SLAB), :])
    rows = jnp.concatenate(rows)
    for y in range(NY):
        out[y] = dot(slabs(held, y), rows, ((0,), (0,))).astype(BF)


def mix_part(place, weight, pieces):
    toks, width = pieces[0].shape[1], weight.shape[2]
    rows = sum(p.shape[0] for p in pieces)
    return call(
        mix_body,
        jax.ShapeDtypeStruct((NY, toks, width), BF),
        [SMEM, VMEM] + [HBM] * len(pieces),
        VMEM,
        2 * rows * toks * width,
        2 * rows * (toks + width),
        fetch_scratch(pieces),
    )(place, weight, *pieces)


def place_body(place, src, dst, taken, given, in_sems, out_sems):
    x, core = place[0], place[1]
    loads = [pltpu.make_async_copy(src.at[y], taken.at[y], in_sems.at[y]) for y in range(NY)]
    for load in loads:
        load.start()
    for load in loads:
        load.wait()
    stores = []
    for i in range(NX * NCORE * NZHI):
        s, c, z = i // (NCORE * NZHI), i // NZHI % NCORE, i % NZHI
        chip = lax.rem(x + NX - s, NX)
        head = (z * NX + chip) * NCORE + (core if c == 0 else 1 - core)
        for y in range(NY):
            given[i, y * SLAB : (y + 1) * SLAB, :] = taken[y, i * SLAB : (i + 1) * SLAB, :]
        stores.append(pltpu.make_async_copy(given.at[i], dst.at[head], out_sems.at[i]))
        stores[-1].start()
    for store in stores:
        store.wait()


def put_heads(place, total):
    heads, width = NX * NCORE * NZHI, total.shape[1]
    return call(
        place_body,
        jax.ShapeDtypeStruct((heads, HEAD, width), BF),
        [SMEM, HBM],
        HBM,
        0,
        4 * total.size,
        [
            pltpu.VMEM((NY, heads * SLAB, width), BF),
            pltpu.VMEM((heads, HEAD, width), BF),
            pltpu.SemaphoreType.DMA((NY,)),
            pltpu.SemaphoreType.DMA((heads,)),
        ],
    )(place, total.reshape(NY, heads * SLAB, width)).reshape(total.shape)


def on_device(
    qkv,
    out_weight,
    cotangent,
    scene_lengths,
    bucket_ids,
    sensor_ids,
    gsd_ids,
    step_ids,
    step_table,
    gsd_table,
    sensor_table,
    bucket_table,
):
    toks = qkv.shape[0]
    width = cotangent.shape[1]
    factor = HEAD ** (-0.5)
    place = jnp.stack([lax.axis_index(a) for a in ("x", "core", "y")]).astype(jnp.int32)
    weight = out_weight.reshape(-1, HEAD, width)

    segments = scene_of(scene_lengths, toks)
    same = segments[:, None] == segments[None, :]
    queries, keys, values = qkv[:, 0], qkv[:, 1], qkv[:, 2]

    scores = dot(queries, keys, ((1,), (1,))) * factor
    scores = jnp.where(same, scores, -1e30)
    top = jnp.max(scores, axis=-1, keepdims=True)
    weights = jnp.exp(scores - top)
    probs = weights / jnp.sum(weights, axis=-1, keepdims=True)
    rounded = probs.astype(BF)
    attended = dot(values, rounded, ((0,), (1,))).astype(BF)

    ids = (step_ids, gsd_ids, sensor_ids, bucket_ids)
    attended, *ids = lax.optimization_barrier((attended, *ids))
    step_ids, gsd_ids, sensor_ids, bucket_ids = ids
    gate_scene = lookup(step_ids, step_table) + lookup(gsd_ids, gsd_table)
    gate_scene = gate_scene + lookup(sensor_ids, sensor_table) + lookup(bucket_ids, bucket_table)
    member = (segments[:, None] == jnp.arange(scene_lengths.shape[0])[None, :]).astype(F32)
    gate = jnp.dot(member, gate_scene, precision=lax.Precision.HIGHEST, preferred_element_type=F32)
    gated = (gate * cotangent.astype(F32)).astype(BF)

    attended, gated = lax.optimization_barrier((attended, gated))
    gated_y = lax.all_gather(gated, "y", axis=0, tiled=True)
    attended = lax.all_to_all(attended, "y", split_axis=0, concat_axis=0, tiled=True)

    sent = upstream_part(place, weight, gated)
    got = shift(sent, "core", NCORE, 1)
    summed = upstream_part(place, weight, gated, got)
    attended, summed = lax.optimization_barrier((attended, summed))
    summed = lax.psum_scatter(summed, "x", scatter_dimension=0, tiled=True)

    own = {0: lax.all_gather(attended, "zhi", axis=0, tiled=True)}
    for s in (1, 3, 2):
        own[s] = shift(own[0], "x", NX, s)
    pieces = [p for s in range(NX) for p in (own[s], shift(own[s], "core", NCORE, 1))]
    *pieces, summed = lax.optimization_barrier((*pieces, summed))

    total = weight_part(pieces, gated_y)
    total = lax.all_gather(total, "zlo").astype(F32).sum(0).astype(BF)
    *pieces, total = lax.optimization_barrier((*pieces, total))
    total = lax.all_gather(total, "y", axis=0, tiled=True)
    total = put_heads(place, total)

    summed = lax.psum_scatter(summed, "zhi", scatter_dimension=0, tiled=True)

    parts = mix_part(place, weight, pieces)
    parts = lax.all_to_all(parts, "y", split_axis=0, concat_axis=0, tiled=True)
    mixed = (gate * parts.astype(F32).sum(0)).astype(BF)

    upstream = summed.T
    grad_values = dot(rounded, upstream, ((0,), (0,))).astype(BF)
    grad_probs = dot(upstream, values, ((1,), (1,)))
    inner = jnp.sum(probs * grad_probs, axis=-1, keepdims=True)
    grad_scores = (probs * (grad_probs - inner)).astype(BF)
    grad_queries = (dot(grad_scores, keys, ((1,), (0,))) * factor).astype(BF)
    grad_keys = (dot(grad_scores, queries, ((0,), (0,))) * factor).astype(BF)
    grad_qkv = jnp.stack([grad_queries, grad_keys, grad_values], axis=1)
    return (mixed, grad_qkv, total)


def solution(mesh):
    fine = Mesh(mesh.devices.reshape(NZLO, NY, NZHI, NX, NCORE), ROW + COL)
    return jax.shard_map(
        on_device,
        mesh=fine,
        in_specs=(
            P(ROW, None, COL),
            P(None, COL),
            P(ROW, COL),
            P(ROW),
            P(ROW),
            P(ROW),
            P(ROW),
            P(ROW),
            P(None, COL),
            P(None, COL),
            P(None, COL),
            P(None, COL),
        ),
        out_specs=(P(ROW, COL), P(ROW, None, COL), P(None, COL)),
        check_vma=False,
    )
```

```python
import jax
import jax.numpy as jnp
from jax import lax
from jax.experimental import pallas as pl
from jax.experimental.pallas import tpu as pltpu
from jax.sharding import Mesh, PartitionSpec as P

HEAD = 128
ROW = ("zlo", "y")
COL = ("zhi", "x", "core")
NZLO, NY, NZHI, NX, NCORE = 3, 8, 4, 4, 2
SLAB = HEAD // NY
F32 = jnp.float32
BF = jnp.bfloat16
SMEM = pl.BlockSpec(memory_space=pltpu.SMEM)
VMEM = pl.BlockSpec(memory_space=pltpu.VMEM)
HBM = pl.BlockSpec(memory_space=pltpu.HBM)


def scene_of(lengths, count):
    ends = jnp.cumsum(lengths)
    places = jnp.arange(count)
    return jnp.sum((places[:, None] >= ends[None, :]).astype(jnp.int32), axis=1)


def lookup(ids, table):
    picks = (ids[:, None] == jnp.arange(table.shape[0])[None, :]).astype(table.dtype)
    return jnp.dot(picks, table, preferred_element_type=F32)


def dot(a, b, dims):
    return lax.dot_general(a, b, (dims, ((), ())), preferred_element_type=F32)


def shift(value, axis, size, step):
    return lax.ppermute(value, axis, [(i, (i + step) % size) for i in range(size)])


def after(value, *others):
    return lax.optimization_barrier((value,) + others)[0]


def call(body, out_shape, in_specs, out_specs, flops, nbytes, scratch=(), limit=60):
    return pl.pallas_call(
        body,
        out_shape=out_shape,
        in_specs=in_specs,
        out_specs=out_specs,
        scratch_shapes=list(scratch),
        compiler_params=pltpu.CompilerParams(vmem_limit_bytes=limit * 1024 * 1024),
        cost_estimate=pl.CostEstimate(flops=flops, bytes_accessed=nbytes, transcendentals=0),
    )


def up_body(place, weight, gated, *refs):
    out = refs[-1]
    core = place[1]
    pick = core if len(refs) == 2 else 1 - core
    for x in range(NX):
        for z in range(NZHI):
            rows = pl.ds((x * NZHI + z) * HEAD, HEAD)
            value = dot(weight[(z * NX + x) * NCORE + pick], gated[...], ((1,), (1,)))
            if len(refs) == 2:
                value = value + refs[0][rows, :].astype(F32)
            out[rows, :] = value.astype(BF)


def upstream_part(place, weight, gated, *got):
    toks = gated.shape[0]
    rows = NX * NZHI * HEAD
    return call(
        up_body,
        jax.ShapeDtypeStruct((rows, toks), BF),
        [SMEM] + [VMEM] * (2 + len(got)),
        VMEM,
        2 * rows * toks * gated.shape[1],
        4 * rows * toks,
        limit=16,
    )(place, weight, gated, *got)


def fetch(pieces, held, sems):
    copies = [pltpu.make_async_copy(p, held.at[i], sems.at[i]) for i, p in enumerate(pieces)]
    for copy in copies:
        copy.start()
    for copy in copies:
        copy.wait()


def slabs(held, y):
    starts = [z * HEAD + y * SLAB for z in range(NZHI)]
    return jnp.concatenate(
        [held[i, start : start + SLAB, :] for i in range(held.shape[0]) for start in starts]
    )


def part_body(*refs):
    *pieces, mine, theirs, out_mine, out_theirs, rows, sems, held = refs
    fetch(pieces, held, sems)
    toks = held.shape[2]
    for y in range(NY):
        rows[:, y * toks : (y + 1) * toks] = slabs(held, y)
    out_theirs[...] = dot(rows[...], theirs[...], ((1,), (0,))).astype(BF)
    out_mine[...] = dot(rows[...], mine[...], ((1,), (0,))).astype(BF)


def weight_part(pieces, mine, theirs):
    rows = sum(p.shape[0] for p in pieces) // NY
    toks, width = mine.shape
    count = len(pieces)
    return call(
        part_body,
        (jax.ShapeDtypeStruct((rows, width), BF),) * 2,
        [HBM] * count + [VMEM] * 2,
        (VMEM, VMEM),
        4 * rows * toks * width,
        2 * rows * toks + 4 * toks * width,
        [
            pltpu.VMEM((rows, toks), BF),
            pltpu.SemaphoreType.DMA((count,)),
            pltpu.VMEM((count, *pieces[0].shape), BF),
        ],
    )(*pieces, mine, theirs)


def mix_body(place, weight, gate, *refs):
    *pieces, out, acc, sems, held = refs
    fetch(pieces, held, sems)
    x, core = place[0], place[1]
    for i in range(len(pieces)):
        s, c = i // 2, i % 2
        chip = lax.rem(x + NX - s, NX)
        pick = core if c == 0 else 1 - core
        rows = jnp.concatenate([weight[(z * NX + chip) * NCORE + pick] for z in range(NZHI)])
        value = dot(held[i], rows, ((0,), (0,)))
        acc[...] = value if i == 0 else acc[...] + value
    out[...] = (gate[...] * acc[...]).astype(BF)


def mix(place, weight, gate, pieces):
    toks, width = gate.shape
    rows = sum(p.shape[0] for p in pieces)
    count = len(pieces)
    return call(
        mix_body,
        jax.ShapeDtypeStruct((toks, width), BF),
        [SMEM] + [VMEM] * 2 + [HBM] * count,
        VMEM,
        2 * rows * toks * width,
        2 * rows * (toks + width),
        [
            pltpu.VMEM((toks, width), F32),
            pltpu.SemaphoreType.DMA((count,)),
            pltpu.VMEM((count, *pieces[0].shape), BF),
        ],
    )(place, weight, gate, *pieces)


def place_body(place, src, dst, taken, given, in_sems, out_sems):
    x, core = place[0], place[1]
    loads = [pltpu.make_async_copy(src.at[y], taken.at[y], in_sems.at[y]) for y in range(NY)]
    for load in loads:
        load.start()
    for load in loads:
        load.wait()
    stores = []
    for i in range(NX * NCORE * NZHI):
        c, s, z = i // (NX * NZHI), i // NZHI % NX, i % NZHI
        chip = lax.rem(x + NX - s, NX)
        head = (z * NX + chip) * NCORE + (core if c == 0 else 1 - core)
        for y in range(NY):
            given[i, y * SLAB : (y + 1) * SLAB, :] = taken[y, i * SLAB : (i + 1) * SLAB, :]
        stores.append(pltpu.make_async_copy(given.at[i], dst.at[head], out_sems.at[i]))
        stores[-1].start()
    for store in stores:
        store.wait()


def put_heads(place, total):
    heads, width = NX * NCORE * NZHI, total.shape[1]
    return call(
        place_body,
        jax.ShapeDtypeStruct((heads, HEAD, width), BF),
        [SMEM, HBM],
        HBM,
        0,
        4 * total.size,
        [
            pltpu.VMEM((NY, heads * SLAB, width), BF),
            pltpu.VMEM((heads, HEAD, width), BF),
            pltpu.SemaphoreType.DMA((NY,)),
            pltpu.SemaphoreType.DMA((heads,)),
        ],
    )(place, total.reshape(NY, heads * SLAB, width)).reshape(total.shape)


def on_device(
    qkv,
    out_weight,
    cotangent,
    scene_lengths,
    bucket_ids,
    sensor_ids,
    gsd_ids,
    step_ids,
    step_table,
    gsd_table,
    sensor_table,
    bucket_table,
):
    toks = qkv.shape[0]
    width = cotangent.shape[1]
    factor = HEAD ** (-0.5)
    place = jnp.stack([lax.axis_index(a) for a in ("x", "core")]).astype(jnp.int32)
    weight = out_weight.reshape(-1, HEAD, width)

    segments = scene_of(scene_lengths, toks)
    same = segments[:, None] == segments[None, :]
    queries, keys, values = qkv[:, 0], qkv[:, 1], qkv[:, 2]

    scores = dot(queries, keys, ((1,), (1,))) * factor
    scores = jnp.where(same, scores, -1e30)
    top = jnp.max(scores, axis=-1, keepdims=True)
    weights = jnp.exp(scores - top)
    probs = weights / jnp.sum(weights, axis=-1, keepdims=True)
    rounded = probs.astype(BF)
    attended = dot(values, rounded, ((0,), (1,))).astype(BF)

    ids = (step_ids, gsd_ids, sensor_ids, bucket_ids)
    attended, *ids = lax.optimization_barrier((attended, *ids))
    step_ids, gsd_ids, sensor_ids, bucket_ids = ids
    gate_scene = lookup(step_ids, step_table) + lookup(gsd_ids, gsd_table)
    gate_scene = gate_scene + lookup(sensor_ids, sensor_table) + lookup(bucket_ids, bucket_table)
    member = (segments[:, None] == jnp.arange(scene_lengths.shape[0])[None, :]).astype(F32)
    gate = jnp.dot(member, gate_scene, precision=lax.Precision.HIGHEST, preferred_element_type=F32)
    gated = (gate * cotangent.astype(F32)).astype(BF)

    attended, gated = lax.optimization_barrier((attended, gated))
    gated_y = lax.all_gather(gated, "y", axis=0, tiled=True)
    natural = attended
    attended = lax.all_to_all(attended, "y", split_axis=0, concat_axis=0, tiled=True)

    sent = upstream_part(place, weight, gated)
    got = shift(sent, "core", NCORE, 1)
    summed = upstream_part(place, weight, gated, got)
    attended, summed = lax.optimization_barrier((attended, summed))
    summed = lax.psum_scatter(summed, "x", scatter_dimension=0, tiled=True)

    own = [lax.all_gather(attended, "zhi", axis=0, tiled=True)]
    gated_y, own[0] = lax.optimization_barrier((gated_y, own[0]))
    own += [shift(own[0], "x", NX, s) for s in (1, 2, 3)]

    theirs_y = shift(gated_y, "core", NCORE, 1)

    total, swap = weight_part(own, gated_y, theirs_y)
    total = jnp.concatenate([total, shift(swap, "core", NCORE, 1)])
    total = lax.all_gather(total, "zlo").astype(F32).sum(0).astype(BF)
    natural, total = lax.optimization_barrier((natural, total))
    total = lax.all_gather(total, "y", axis=0, tiled=True)
    total = put_heads(place, total)

    summed = lax.psum_scatter(summed, "zhi", scatter_dimension=0, tiled=True)

    whole = [lax.all_gather(natural, "zhi", axis=0, tiled=True)]
    whole += [shift(whole[0], "x", NX, s) for s in (1, 2, 3)]
    mixed = mix(place, weight, gate, [p for w in whole for p in (w, shift(w, "core", NCORE, 1))])

    upstream = summed.T
    grad_values = dot(rounded, upstream, ((0,), (0,))).astype(BF)
    grad_probs = dot(upstream, values, ((1,), (1,)))
    inner = jnp.sum(probs * grad_probs, axis=-1, keepdims=True)
    grad_scores = (probs * (grad_probs - inner)).astype(BF)
    grad_queries = (dot(grad_scores, keys, ((1,), (0,))) * factor).astype(BF)
    grad_keys = (dot(grad_scores, queries, ((0,), (0,))) * factor).astype(BF)
    grad_qkv = jnp.stack([grad_queries, grad_keys, grad_values], axis=1)
    return (mixed, grad_qkv, total)


def solution(mesh):
    fine = Mesh(mesh.devices.reshape(NZLO, NY, NZHI, NX, NCORE), ROW + COL)
    return jax.shard_map(
        on_device,
        mesh=fine,
        in_specs=(
            P(ROW, None, COL),
            P(None, COL),
            P(ROW, COL),
            P(ROW),
            P(ROW),
            P(ROW),
            P(ROW),
            P(ROW),
            P(None, COL),
            P(None, COL),
            P(None, COL),
            P(None, COL),
        ),
        out_specs=(P(ROW, COL), P(ROW, None, COL), P(None, COL)),
        check_vma=False,
    )
```

```python
import jax
import jax.numpy as jnp
from jax import lax
from jax.experimental import pallas as pl
from jax.experimental.pallas import tpu as pltpu
from jax.sharding import Mesh, PartitionSpec as P

HEAD = 128
ROW = ("zlo", "y")
COL = ("zhi", "x", "core")
NZLO, NY, NZHI, NX, NCORE = 3, 8, 4, 4, 2
SLAB = HEAD // NY
F32 = jnp.float32
BF = jnp.bfloat16
SMEM = pl.BlockSpec(memory_space=pltpu.SMEM)
VMEM = pl.BlockSpec(memory_space=pltpu.VMEM)
HBM = pl.BlockSpec(memory_space=pltpu.HBM)


def scene_of(lengths, count):
    ends = jnp.cumsum(lengths)
    places = jnp.arange(count)
    return jnp.sum((places[:, None] >= ends[None, :]).astype(jnp.int32), axis=1)


def lookup(ids, table):
    picks = (ids[:, None] == jnp.arange(table.shape[0])[None, :]).astype(table.dtype)
    return jnp.dot(picks, table, preferred_element_type=F32)


def dot(a, b, dims):
    return lax.dot_general(a, b, (dims, ((), ())), preferred_element_type=F32)


def shift(value, axis, size, step):
    return lax.ppermute(value, axis, [(i, (i + step) % size) for i in range(size)])


def after(value, *others):
    return lax.optimization_barrier((value,) + others)[0]


def call(body, out_shape, in_specs, out_specs, flops, nbytes, scratch=(), limit=60):
    return pl.pallas_call(
        body,
        out_shape=out_shape,
        in_specs=in_specs,
        out_specs=out_specs,
        scratch_shapes=list(scratch),
        compiler_params=pltpu.CompilerParams(vmem_limit_bytes=limit * 1024 * 1024),
        cost_estimate=pl.CostEstimate(flops=flops, bytes_accessed=nbytes, transcendentals=0),
    )


def up_body(place, weight, other, gated, theirs, out):
    core = place[1]
    for x in range(NX):
        for z in range(NZHI):
            head = z * NX + x
            value = dot(weight[head * NCORE + core], gated[...], ((1,), (1,)))
            value = value + dot(other[head], theirs[...], ((1,), (1,)))
            rows = pl.ds((x * NZHI + z) * HEAD, HEAD)
            out[rows, :] = value.astype(BF)


def upstream_part(place, weight, other, gated, theirs):
    toks = gated.shape[0]
    rows = NX * NZHI * HEAD
    return call(
        up_body,
        jax.ShapeDtypeStruct((rows, toks), BF),
        [SMEM] + [VMEM] * 4,
        VMEM,
        4 * rows * toks * gated.shape[1],
        4 * rows * toks,
        limit=16,
    )(place, weight, other, gated, theirs)


def fetch(pieces, held, sems):
    copies = [pltpu.make_async_copy(p, held.at[i], sems.at[i]) for i, p in enumerate(pieces)]
    for copy in copies:
        copy.start()
    for copy in copies:
        copy.wait()


def slabs(held, y):
    starts = [z * HEAD + y * SLAB for z in range(NZHI)]
    return jnp.concatenate(
        [held[i, start : start + SLAB, :] for i in range(held.shape[0]) for start in starts]
    )


def part_body(*refs):
    *pieces, mine, theirs, out_mine, out_theirs, rows, sems, held = refs
    fetch(pieces, held, sems)
    toks = held.shape[2]
    for y in range(NY):
        rows[:, y * toks : (y + 1) * toks] = slabs(held, y)
    out_theirs[...] = dot(rows[...], theirs[...], ((1,), (0,))).astype(BF)
    out_mine[...] = dot(rows[...], mine[...], ((1,), (0,))).astype(BF)


def weight_part(pieces, mine, theirs):
    rows = sum(p.shape[0] for p in pieces) // NY
    toks, width = mine.shape
    count = len(pieces)
    return call(
        part_body,
        (jax.ShapeDtypeStruct((rows, width), BF),) * 2,
        [HBM] * count + [VMEM] * 2,
        (VMEM, VMEM),
        4 * rows * toks * width,
        2 * rows * toks + 4 * toks * width,
        [
            pltpu.VMEM((rows, toks), BF),
            pltpu.SemaphoreType.DMA((count,)),
            pltpu.VMEM((count, *pieces[0].shape), BF),
        ],
    )(*pieces, mine, theirs)


def mix_body(place, weight, other, *refs):
    *pieces, out_mine, out_theirs, sems, held = refs
    fetch(pieces, held, sems)
    x, core = place[0], place[1]
    for mine in (False, True):
        rows = []
        for s in range(len(pieces)):
            chip = lax.rem(x + NX - s, NX)
            for z in range(NZHI):
                head = z * NX + chip
                rows.append(weight[head * NCORE + core] if mine else other[head])
        value = dot(held[...].reshape(-1, held.shape[2]), jnp.concatenate(rows), ((0,), (0,)))
        if mine:
            out_mine[...] = value
        else:
            out_theirs[...] = value.astype(BF)


def mix_part(place, weight, other, pieces):
    toks, width = pieces[0].shape[1], weight.shape[2]
    rows = sum(p.shape[0] for p in pieces)
    count = len(pieces)
    return call(
        mix_body,
        (
            jax.ShapeDtypeStruct((toks, width), F32),
            jax.ShapeDtypeStruct((toks, width), BF),
        ),
        [SMEM] + [VMEM] * 2 + [HBM] * count,
        (VMEM, VMEM),
        4 * rows * toks * width,
        2 * rows * (toks + 2 * width),
        [
            pltpu.SemaphoreType.DMA((count,)),
            pltpu.VMEM((count, *pieces[0].shape), BF),
        ],
    )(place, weight, other, *pieces)


def place_body(place, src, dst, taken, given, in_sems, out_sems):
    x, core = place[0], place[1]
    loads = [pltpu.make_async_copy(src.at[y], taken.at[y], in_sems.at[y]) for y in range(NY)]
    for load in loads:
        load.start()
    for load in loads:
        load.wait()
    stores = []
    for i in range(NX * NCORE * NZHI):
        c, s, z = i // (NX * NZHI), i // NZHI % NX, i % NZHI
        chip = lax.rem(x + NX - s, NX)
        head = (z * NX + chip) * NCORE + (core if c == 0 else 1 - core)
        for y in range(NY):
            given[i, y * SLAB : (y + 1) * SLAB, :] = taken[y, i * SLAB : (i + 1) * SLAB, :]
        stores.append(pltpu.make_async_copy(given.at[i], dst.at[head], out_sems.at[i]))
        stores[-1].start()
    for store in stores:
        store.wait()


def put_heads(place, total):
    heads, width = NX * NCORE * NZHI, total.shape[1]
    return call(
        place_body,
        jax.ShapeDtypeStruct((heads, HEAD, width), BF),
        [SMEM, HBM],
        HBM,
        0,
        4 * total.size,
        [
            pltpu.VMEM((NY, heads * SLAB, width), BF),
            pltpu.VMEM((heads, HEAD, width), BF),
            pltpu.SemaphoreType.DMA((NY,)),
            pltpu.SemaphoreType.DMA((heads,)),
        ],
    )(place, total.reshape(NY, heads * SLAB, width)).reshape(total.shape)


def on_device(
    qkv,
    out_weight,
    cotangent,
    scene_lengths,
    bucket_ids,
    sensor_ids,
    gsd_ids,
    step_ids,
    step_table,
    gsd_table,
    sensor_table,
    bucket_table,
):
    toks = qkv.shape[0]
    width = cotangent.shape[1]
    factor = HEAD ** (-0.5)
    place = jnp.stack([lax.axis_index(a) for a in ("x", "core")]).astype(jnp.int32)
    weight = out_weight.reshape(-1, HEAD, width)

    other = weight.reshape(-1, NCORE, HEAD, width)
    other = lax.dynamic_index_in_dim(other, 1 - place[1], 1, keepdims=False)
    other = shift(other, "core", NCORE, 1)

    segments = scene_of(scene_lengths, toks)
    same = segments[:, None] == segments[None, :]
    queries, keys, values = qkv[:, 0], qkv[:, 1], qkv[:, 2]

    scores = dot(queries, keys, ((1,), (1,))) * factor
    scores = jnp.where(same, scores, -1e30)
    top = jnp.max(scores, axis=-1, keepdims=True)
    weights = jnp.exp(scores - top)
    probs = weights / jnp.sum(weights, axis=-1, keepdims=True)
    rounded = probs.astype(BF)
    attended = dot(values, rounded, ((0,), (1,))).astype(BF)

    ids = (step_ids, gsd_ids, sensor_ids, bucket_ids)
    attended, *ids = lax.optimization_barrier((attended, *ids))
    step_ids, gsd_ids, sensor_ids, bucket_ids = ids
    gate_scene = lookup(step_ids, step_table) + lookup(gsd_ids, gsd_table)
    gate_scene = gate_scene + lookup(sensor_ids, sensor_table) + lookup(bucket_ids, bucket_table)
    member = (segments[:, None] == jnp.arange(scene_lengths.shape[0])[None, :]).astype(F32)
    gate = jnp.dot(member, gate_scene, precision=lax.Precision.HIGHEST, preferred_element_type=F32)
    gated = (gate * cotangent.astype(F32)).astype(BF)

    attended, gated = lax.optimization_barrier((attended, gated))
    gated_y = lax.all_gather(gated, "y", axis=0, tiled=True)
    natural = attended
    attended = lax.all_to_all(attended, "y", split_axis=0, concat_axis=0, tiled=True)

    summed = upstream_part(place, weight, other, gated, shift(gated, "core", NCORE, 1))
    attended, summed = lax.optimization_barrier((attended, summed))
    summed = lax.psum_scatter(summed, "x", scatter_dimension=0, tiled=True)

    own = [lax.all_gather(attended, "zhi", axis=0, tiled=True)]
    gated_y, own[0] = lax.optimization_barrier((gated_y, own[0]))
    own += [shift(own[0], "x", NX, s) for s in (1, 2, 3)]
    theirs_y = shift(gated_y, "core", NCORE, 1)

    total, swap = weight_part(own, gated_y, theirs_y)
    total = jnp.concatenate([total, shift(swap, "core", NCORE, 1)])
    total = lax.all_gather(total, "zlo").astype(F32).sum(0).astype(BF)
    natural, total = lax.optimization_barrier((natural, total))
    total = lax.all_gather(total, "y", axis=0, tiled=True)
    total = put_heads(place, total)

    summed = lax.psum_scatter(summed, "zhi", scatter_dimension=0, tiled=True)

    whole = [lax.all_gather(natural, "zhi", axis=0, tiled=True)]
    whole += [shift(whole[0], "x", NX, s) for s in (1, 2, 3)]
    upstream = summed.T
    grad_values = dot(rounded, upstream, ((0,), (0,))).astype(BF)
    grad_probs = dot(upstream, values, ((1,), (1,)))
    inner = jnp.sum(probs * grad_probs, axis=-1, keepdims=True)
    grad_scores = (probs * (grad_probs - inner)).astype(BF)
    grad_queries = (dot(grad_scores, keys, ((1,), (0,))) * factor).astype(BF)
    grad_keys = (dot(grad_scores, queries, ((0,), (0,))) * factor).astype(BF)
    grad_qkv = jnp.stack([grad_queries, grad_keys, grad_values], axis=1)

    *whole, grad_qkv = lax.optimization_barrier((*whole, grad_qkv))
    mixed, swap = mix_part(place, weight, other, whole)
    mixed = (gate * (mixed + shift(swap, "core", NCORE, 1).astype(F32))).astype(BF)
    return (mixed, grad_qkv, total)


def solution(mesh):
    fine = Mesh(mesh.devices.reshape(NZLO, NY, NZHI, NX, NCORE), ROW + COL)
    return jax.shard_map(
        on_device,
        mesh=fine,
        in_specs=(
            P(ROW, None, COL),
            P(None, COL),
            P(ROW, COL),
            P(ROW),
            P(ROW),
            P(ROW),
            P(ROW),
            P(ROW),
            P(None, COL),
            P(None, COL),
            P(None, COL),
            P(None, COL),
        ),
        out_specs=(P(ROW, COL), P(ROW, None, COL), P(None, COL)),
        check_vma=False,
    )
```

```python
import jax
import jax.numpy as jnp
from jax import lax
from jax.experimental import pallas as pl
from jax.experimental.layout import Layout, with_layout_constraint
from jax.experimental.pallas import tpu as pltpu
from jax.sharding import Mesh, PartitionSpec as P

HEAD = 128
ROW = ("zlo", "y")
COL = ("zhi", "x", "core")
NZLO, NY, NZHI, NX, NCORE = 3, 8, 4, 4, 2
SLAB = HEAD // NY
F32 = jnp.float32
BF = jnp.bfloat16
SMEM = pl.BlockSpec(memory_space=pltpu.SMEM)
VMEM = pl.BlockSpec(memory_space=pltpu.VMEM)
HBM = pl.BlockSpec(memory_space=pltpu.HBM)


def scene_of(lengths, count):
    ends = jnp.cumsum(lengths)
    places = jnp.arange(count)
    return jnp.sum((places[:, None] >= ends[None, :]).astype(jnp.int32), axis=1)


def lookup(ids, table):
    picks = (ids[:, None] == jnp.arange(table.shape[0])[None, :]).astype(table.dtype)
    return jnp.dot(picks, table, preferred_element_type=F32)


def dot(a, b, dims):
    return lax.dot_general(a, b, (dims, ((), ())), preferred_element_type=F32)


def shift(value, axis, size, step):
    return lax.ppermute(value, axis, [(i, (i + step) % size) for i in range(size)])


def gather_x(value):
    return lax.all_to_all(value, "x", split_axis=0, concat_axis=0, tiled=True)


def after(value, *others):
    return lax.optimization_barrier((value,) + others)[0]


def call(body, out_shape, in_specs, out_specs, flops, nbytes, scratch=(), limit=60):
    return pl.pallas_call(
        body,
        out_shape=out_shape,
        in_specs=in_specs,
        out_specs=out_specs,
        scratch_shapes=list(scratch),
        compiler_params=pltpu.CompilerParams(vmem_limit_bytes=limit * 1024 * 1024),
        cost_estimate=pl.CostEstimate(flops=flops, bytes_accessed=nbytes, transcendentals=0),
    )


def up_body(place, weight, other, gated, theirs, out):
    core = place[0]
    for x in range(NX):
        for z in range(NZHI):
            head = z * NX + x
            value = dot(weight[head * NCORE + core], gated[...], ((1,), (1,)))
            value = value + dot(other[head], theirs[...], ((1,), (1,)))
            rows = pl.ds((x * NZHI + z) * HEAD, HEAD)
            out[rows, :] = value.astype(BF)


def upstream_part(place, weight, other, gated, theirs):
    toks = gated.shape[0]
    rows = NX * NZHI * HEAD
    return call(
        up_body,
        jax.ShapeDtypeStruct((rows, toks), BF),
        [SMEM] + [VMEM] * 4,
        VMEM,
        4 * rows * toks * gated.shape[1],
        4 * rows * toks,
        limit=16,
    )(place, weight, other, gated, theirs)


def slabs(held, y):
    starts = [h * HEAD + y * SLAB for h in range(held.shape[0] // HEAD)]
    return jnp.concatenate([held[start : start + SLAB, :] for start in starts])


def part_body(held, mine, theirs, out_mine, out_theirs, rows):
    toks = held.shape[1]
    for y in range(NY):
        rows[:, y * toks : (y + 1) * toks] = slabs(held, y)
    out_theirs[...] = dot(rows[...], theirs[...], ((1,), (0,))).astype(BF)
    out_mine[...] = dot(rows[...], mine[...], ((1,), (0,))).astype(BF)


def weight_part(held, mine, theirs):
    rows = held.shape[0] // NY
    toks, width = mine.shape
    return call(
        part_body,
        (jax.ShapeDtypeStruct((rows, width), BF),) * 2,
        [VMEM] * 3,
        (VMEM, VMEM),
        4 * rows * toks * width,
        2 * rows * toks + 4 * toks * width,
        [pltpu.VMEM((rows, toks), BF)],
        limit=16,
    )(held, mine, theirs)


def mix_body(place, weight, other, held, out_mine, out_theirs):
    core = place[0]
    heads = [z * NX + x for x in range(NX) for z in range(NZHI)]
    theirs = jnp.concatenate([other[head] for head in heads])
    out_theirs[...] = dot(held[...], theirs, ((0,), (0,))).astype(BF)
    mine = jnp.concatenate([weight[head * NCORE + core] for head in heads])
    out_mine[...] = dot(held[...], mine, ((0,), (0,)))


def mix_part(place, weight, other, held):
    rows, toks = held.shape
    width = weight.shape[2]
    return call(
        mix_body,
        (
            jax.ShapeDtypeStruct((toks, width), F32),
            jax.ShapeDtypeStruct((toks, width), BF),
        ),
        [SMEM] + [VMEM] * 3,
        (VMEM, VMEM),
        4 * rows * toks * width,
        2 * rows * (toks + 2 * width),
        limit=16,
    )(place, weight, other, held)


def place_body(place, src, dst, taken, given, in_sems, out_sems):
    core = place[0]
    loads = [pltpu.make_async_copy(src.at[y], taken.at[y], in_sems.at[y]) for y in range(NY)]
    for load in loads:
        load.start()
    for load in loads:
        load.wait()
    stores = []
    for i in range(NX * NCORE * NZHI):
        c, x, z = i // (NX * NZHI), i // NZHI % NX, i % NZHI
        head = (z * NX + x) * NCORE + (core if c == 0 else 1 - core)
        for y in range(NY):
            given[i, y * SLAB : (y + 1) * SLAB, :] = taken[y, i * SLAB : (i + 1) * SLAB, :]
        stores.append(pltpu.make_async_copy(given.at[i], dst.at[head], out_sems.at[i]))
        stores[-1].start()
    for store in stores:
        store.wait()


def put_heads(place, total):
    heads, width = NX * NCORE * NZHI, total.shape[1]
    return call(
        place_body,
        jax.ShapeDtypeStruct((heads, HEAD, width), BF),
        [SMEM, HBM],
        HBM,
        0,
        4 * total.size,
        [
            pltpu.VMEM((NY, heads * SLAB, width), BF),
            pltpu.VMEM((heads, HEAD, width), BF),
            pltpu.SemaphoreType.DMA((NY,)),
            pltpu.SemaphoreType.DMA((heads,)),
        ],
    )(place, total.reshape(NY, heads * SLAB, width)).reshape(total.shape)


def on_device(
    qkv,
    out_weight,
    cotangent,
    scene_lengths,
    bucket_ids,
    sensor_ids,
    gsd_ids,
    step_ids,
    step_table,
    gsd_table,
    sensor_table,
    bucket_table,
):
    toks = qkv.shape[0]
    width = cotangent.shape[1]
    factor = HEAD ** (-0.5)
    core = lax.axis_index("core")
    place = core.reshape(1).astype(jnp.int32)
    weight = out_weight.reshape(-1, HEAD, width)

    other = weight.reshape(-1, NCORE, HEAD, width)
    other = lax.dynamic_index_in_dim(other, 1 - core, 1, keepdims=False)
    other = shift(other, "core", NCORE, 1)

    segments = scene_of(scene_lengths, toks)
    same = segments[:, None] == segments[None, :]
    queries, keys, values = qkv[:, 0], qkv[:, 1], qkv[:, 2]

    scores = dot(queries, keys, ((1,), (1,))) * factor
    scores = jnp.where(same, scores, -1e30)
    top = jnp.max(scores, axis=-1, keepdims=True)
    weights = jnp.exp(scores - top)
    probs = weights / jnp.sum(weights, axis=-1, keepdims=True)
    rounded = probs.astype(BF)
    attended = dot(values, rounded, ((0,), (1,))).astype(BF)
    attended = with_layout_constraint(attended, Layout((0, 1)))

    ids = (step_ids, gsd_ids, sensor_ids, bucket_ids)
    attended, *ids = lax.optimization_barrier((attended, *ids))
    step_ids, gsd_ids, sensor_ids, bucket_ids = ids
    gate_scene = lookup(step_ids, step_table) + lookup(gsd_ids, gsd_table)
    gate_scene = gate_scene + lookup(sensor_ids, sensor_table) + lookup(bucket_ids, bucket_table)
    member = (segments[:, None] == jnp.arange(scene_lengths.shape[0])[None, :]).astype(F32)
    gate = jnp.dot(member, gate_scene, precision=lax.Precision.HIGHEST, preferred_element_type=F32)
    gated = (gate * cotangent.astype(F32)).astype(BF)

    attended, gated = lax.optimization_barrier((attended, gated))
    gated_y = lax.all_gather(gated, "y", axis=0, tiled=True)
    natural = attended
    attended = lax.all_to_all(attended, "y", split_axis=0, concat_axis=0, tiled=True)

    summed = upstream_part(place, weight, other, gated, shift(gated, "core", NCORE, 1))
    attended, summed = lax.optimization_barrier((attended, summed))
    summed = lax.psum_scatter(summed, "x", scatter_dimension=0, tiled=True)

    own = lax.all_gather(attended, "zhi", axis=0, tiled=True)
    own = jnp.concatenate([own] * NX)
    gated_y = after(gated_y, own)
    own = gather_x(own)
    theirs_y = shift(gated_y, "core", NCORE, 1)

    total, swap = weight_part(own, gated_y, theirs_y)
    total = jnp.concatenate([total, shift(swap, "core", NCORE, 1)])
    total = lax.all_gather(total, "zlo").astype(F32).sum(0).astype(BF)
    natural, total = lax.optimization_barrier((natural, total))
    total = lax.all_gather(total, "y", axis=0, tiled=True)
    total = put_heads(place, total)

    summed = lax.psum_scatter(summed, "zhi", scatter_dimension=0, tiled=True)

    whole = lax.all_gather(natural, "zhi", axis=0, tiled=True)
    whole = gather_x(jnp.concatenate([whole] * NX))

    upstream = summed.T
    grad_values = dot(rounded, upstream, ((0,), (0,))).astype(BF)
    grad_probs = dot(upstream, values, ((1,), (1,)))
    inner = jnp.sum(probs * grad_probs, axis=-1, keepdims=True)
    grad_scores = (probs * (grad_probs - inner)).astype(BF)
    grad_queries = (dot(grad_scores, keys, ((1,), (0,))) * factor).astype(BF)
    grad_keys = (dot(grad_scores, queries, ((0,), (0,))) * factor).astype(BF)
    grad_qkv = jnp.stack([grad_queries, grad_keys, grad_values], axis=1)

    whole, grad_qkv = lax.optimization_barrier((whole, grad_qkv))
    mixed, swap = mix_part(place, weight, other, whole)
    mixed = (gate * (mixed + shift(swap, "core", NCORE, 1).astype(F32))).astype(BF)
    return (mixed, grad_qkv, total)


def solution(mesh):
    fine = Mesh(mesh.devices.reshape(NZLO, NY, NZHI, NX, NCORE), ROW + COL)
    return jax.shard_map(
        on_device,
        mesh=fine,
        in_specs=(
            P(ROW, None, COL),
            P(None, COL),
            P(ROW, COL),
            P(ROW),
            P(ROW),
            P(ROW),
            P(ROW),
            P(ROW),
            P(None, COL),
            P(None, COL),
            P(None, COL),
            P(None, COL),
        ),
        out_specs=(P(ROW, COL), P(ROW, None, COL), P(None, COL)),
        check_vma=False,
    )
```

```python
import jax
import jax.numpy as jnp
from jax import lax
from jax.experimental import pallas as pl
from jax.experimental.layout import Layout, with_layout_constraint
from jax.experimental.pallas import tpu as pltpu
from jax.sharding import Mesh, PartitionSpec as P

HEAD = 128
ROW = ("zlo", "y")
COL = ("zhi", "x", "core")
NZLO, NY, NZHI, NX, NCORE = 3, 8, 4, 4, 2
SLAB = HEAD // NY
F32 = jnp.float32
BF = jnp.bfloat16
SMEM = pl.BlockSpec(memory_space=pltpu.SMEM)
VMEM = pl.BlockSpec(memory_space=pltpu.VMEM)
HBM = pl.BlockSpec(memory_space=pltpu.HBM)


def scene_of(lengths, count):
    ends = jnp.cumsum(lengths)
    places = jnp.arange(count)
    return jnp.sum((places[:, None] >= ends[None, :]).astype(jnp.int32), axis=1)


def lookup(ids, table):
    picks = (ids[:, None] == jnp.arange(table.shape[0])[None, :]).astype(table.dtype)
    return jnp.dot(picks, table, preferred_element_type=F32)


def dot(a, b, dims):
    return lax.dot_general(a, b, (dims, ((), ())), preferred_element_type=F32)


def shift(value, axis, size, step):
    return lax.ppermute(value, axis, [(i, (i + step) % size) for i in range(size)])


def gather_x(value):
    return lax.all_to_all(value, "x", split_axis=0, concat_axis=0, tiled=True)


def after(value, *others):
    return lax.optimization_barrier((value,) + others)[0]


def call(body, out_shape, in_specs, out_specs, flops, nbytes, scratch=(), limit=60):
    return pl.pallas_call(
        body,
        out_shape=out_shape,
        in_specs=in_specs,
        out_specs=out_specs,
        scratch_shapes=list(scratch),
        compiler_params=pltpu.CompilerParams(vmem_limit_bytes=limit * 1024 * 1024),
        cost_estimate=pl.CostEstimate(flops=flops, bytes_accessed=nbytes, transcendentals=0),
    )


def up_body(place, weight, other, gated, theirs, out):
    core = place[0]
    for x in range(NX):
        for z in range(NZHI):
            head = z * NX + x
            value = dot(weight[head * NCORE + core], gated[...], ((1,), (1,)))
            value = value + dot(other[head], theirs[...], ((1,), (1,)))
            rows = pl.ds((x * NZHI + z) * HEAD, HEAD)
            out[rows, :] = value.astype(BF)


def upstream_part(place, weight, other, gated, theirs):
    toks = gated.shape[0]
    rows = NX * NZHI * HEAD
    return call(
        up_body,
        jax.ShapeDtypeStruct((rows, toks), BF),
        [SMEM] + [VMEM] * 4,
        VMEM,
        4 * rows * toks * gated.shape[1],
        4 * rows * toks,
        limit=16,
    )(place, weight, other, gated, theirs)


def slabs(held, y):
    starts = [h * HEAD + y * SLAB for h in range(held.shape[0] // HEAD)]
    return jnp.concatenate([held[start : start + SLAB, :] for start in starts])


def part_body(held, mine, theirs, out_mine, out_theirs, rows):
    toks = held.shape[1]
    for y in range(NY):
        rows[:, y * toks : (y + 1) * toks] = slabs(held, y)
    out_theirs[...] = dot(rows[...], theirs[...], ((1,), (0,))).astype(BF)
    out_mine[...] = dot(rows[...], mine[...], ((1,), (0,))).astype(BF)


def weight_part(held, mine, theirs):
    rows = held.shape[0] // NY
    toks, width = mine.shape
    return call(
        part_body,
        (jax.ShapeDtypeStruct((rows, width), BF),) * 2,
        [VMEM] * 3,
        (VMEM, VMEM),
        4 * rows * toks * width,
        2 * rows * toks + 4 * toks * width,
        [pltpu.VMEM((rows, toks), BF)],
        limit=16,
    )(held, mine, theirs)


def mix_body(place, weight, other, *refs):
    *pieces, out_mine, out_theirs = refs
    core, x = place[0], place[1]
    held = jnp.concatenate([piece[...] for piece in pieces])
    heads = []
    for i in range(NX):
        chip = lax.rem(x + NX - i, NX)
        heads += [z * NX + chip for z in range(NZHI)]
    theirs = jnp.concatenate([other[head] for head in heads])
    out_theirs[...] = dot(held, theirs, ((0,), (0,))).astype(BF)
    mine = jnp.concatenate([weight[head * NCORE + core] for head in heads])
    out_mine[...] = dot(held, mine, ((0,), (0,)))


def mix_part(place, weight, other, pieces):
    toks, width = pieces[0].shape[1], weight.shape[2]
    rows = sum(p.shape[0] for p in pieces)
    return call(
        mix_body,
        (
            jax.ShapeDtypeStruct((toks, width), F32),
            jax.ShapeDtypeStruct((toks, width), BF),
        ),
        [SMEM] + [VMEM] * (2 + len(pieces)),
        (VMEM, VMEM),
        4 * rows * toks * width,
        2 * rows * (toks + 2 * width),
        limit=16,
    )(place, weight, other, *pieces)


def place_body(place, src, dst, taken, given, in_sems, out_sems):
    core = place[0]
    loads = [pltpu.make_async_copy(src.at[y], taken.at[y], in_sems.at[y]) for y in range(NY)]
    for load in loads:
        load.start()
    for load in loads:
        load.wait()
    stores = []
    for i in range(NX * NCORE * NZHI):
        c, x, z = i // (NX * NZHI), i // NZHI % NX, i % NZHI
        head = (z * NX + x) * NCORE + (core if c == 0 else 1 - core)
        for y in range(NY):
            given[i, y * SLAB : (y + 1) * SLAB, :] = taken[y, i * SLAB : (i + 1) * SLAB, :]
        stores.append(pltpu.make_async_copy(given.at[i], dst.at[head], out_sems.at[i]))
        stores[-1].start()
    for store in stores:
        store.wait()


def put_heads(place, total):
    heads, width = NX * NCORE * NZHI, total.shape[1]
    return call(
        place_body,
        jax.ShapeDtypeStruct((heads, HEAD, width), BF),
        [SMEM, HBM],
        HBM,
        0,
        4 * total.size,
        [
            pltpu.VMEM((NY, heads * SLAB, width), BF),
            pltpu.VMEM((heads, HEAD, width), BF),
            pltpu.SemaphoreType.DMA((NY,)),
            pltpu.SemaphoreType.DMA((heads,)),
        ],
    )(place, total.reshape(NY, heads * SLAB, width)).reshape(total.shape)


def on_device(
    qkv,
    out_weight,
    cotangent,
    scene_lengths,
    bucket_ids,
    sensor_ids,
    gsd_ids,
    step_ids,
    step_table,
    gsd_table,
    sensor_table,
    bucket_table,
):
    toks = qkv.shape[0]
    width = cotangent.shape[1]
    factor = HEAD ** (-0.5)
    core = lax.axis_index("core")
    place = jnp.stack([core, lax.axis_index("x")]).astype(jnp.int32)
    weight = out_weight.reshape(-1, HEAD, width)

    other = weight.reshape(-1, NCORE, HEAD, width)
    other = lax.dynamic_index_in_dim(other, 1 - core, 1, keepdims=False)
    other = shift(other, "core", NCORE, 1)

    segments = scene_of(scene_lengths, toks)
    same = segments[:, None] == segments[None, :]
    queries, keys, values = qkv[:, 0], qkv[:, 1], qkv[:, 2]

    scores = dot(queries, keys, ((1,), (1,))) * factor
    scores = jnp.where(same, scores, -1e30)
    top = jnp.max(scores, axis=-1, keepdims=True)
    weights = jnp.exp(scores - top)
    probs = weights / jnp.sum(weights, axis=-1, keepdims=True)
    rounded = probs.astype(BF)
    attended = dot(values, rounded, ((0,), (1,))).astype(BF)
    attended = with_layout_constraint(attended, Layout((0, 1)))

    ids = (step_ids, gsd_ids, sensor_ids, bucket_ids)
    attended, *ids = lax.optimization_barrier((attended, *ids))
    step_ids, gsd_ids, sensor_ids, bucket_ids = ids
    gate_scene = lookup(step_ids, step_table) + lookup(gsd_ids, gsd_table)
    gate_scene = gate_scene + lookup(sensor_ids, sensor_table) + lookup(bucket_ids, bucket_table)
    member = (segments[:, None] == jnp.arange(scene_lengths.shape[0])[None, :]).astype(F32)
    gate = jnp.dot(member, gate_scene, precision=lax.Precision.HIGHEST, preferred_element_type=F32)
    gated = (gate * cotangent.astype(F32)).astype(BF)

    attended, gated = lax.optimization_barrier((attended, gated))
    gated_y = lax.all_gather(gated, "y", axis=0, tiled=True)
    natural = attended
    attended = lax.all_to_all(attended, "y", split_axis=0, concat_axis=0, tiled=True)

    summed = upstream_part(place, weight, other, gated, shift(gated, "core", NCORE, 1))
    attended, summed = lax.optimization_barrier((attended, summed))
    summed = lax.psum_scatter(summed, "x", scatter_dimension=0, tiled=True)

    own = lax.all_gather(attended, "zhi", axis=0, tiled=True)
    own = jnp.concatenate([own] * NX)
    gated_y = after(gated_y, own)
    natural = after(natural, own)
    own = gather_x(own)

    whole = lax.all_gather(natural, "zhi", axis=0, tiled=True)
    own, whole = lax.optimization_barrier((own, whole))
    theirs_y = shift(gated_y, "core", NCORE, 1)

    total, swap = weight_part(own, gated_y, theirs_y)
    total = jnp.concatenate([total, shift(swap, "core", NCORE, 1)])
    total = lax.all_gather(total, "zlo").astype(F32).sum(0).astype(BF)
    whole = after(whole, total)
    summed = after(summed, total)
    total = lax.all_gather(total, "y", axis=0, tiled=True)
    total = put_heads(place, total)

    summed = lax.all_to_all(summed, "zhi", split_axis=0, concat_axis=0, tiled=True)
    summed = summed.reshape(NZHI, HEAD, toks).astype(F32).sum(0).astype(BF)

    whole = [whole] + [shift(whole, "x", NX, i) for i in (1, 2, 3)]

    upstream = summed.T
    grad_values = dot(rounded, upstream, ((0,), (0,))).astype(BF)
    grad_probs = dot(upstream, values, ((1,), (1,)))
    inner = jnp.sum(probs * grad_probs, axis=-1, keepdims=True)
    grad_scores = (probs * (grad_probs - inner)).astype(BF)
    grad_queries = (dot(grad_scores, keys, ((1,), (0,))) * factor).astype(BF)
    grad_keys = (dot(grad_scores, queries, ((0,), (0,))) * factor).astype(BF)
    grad_qkv = jnp.stack([grad_queries, grad_keys, grad_values], axis=1)

    *whole, grad_qkv = lax.optimization_barrier((*whole, grad_qkv))
    mixed, swap = mix_part(place, weight, other, whole)
    mixed = (gate * (mixed + shift(swap, "core", NCORE, 1).astype(F32))).astype(BF)
    return (mixed, grad_qkv, total)


def solution(mesh):
    fine = Mesh(mesh.devices.reshape(NZLO, NY, NZHI, NX, NCORE), ROW + COL)
    return jax.shard_map(
        on_device,
        mesh=fine,
        in_specs=(
            P(ROW, None, COL),
            P(None, COL),
            P(ROW, COL),
            P(ROW),
            P(ROW),
            P(ROW),
            P(ROW),
            P(ROW),
            P(None, COL),
            P(None, COL),
            P(None, COL),
            P(None, COL),
        ),
        out_specs=(P(ROW, COL), P(ROW, None, COL), P(None, COL)),
        check_vma=False,
    )
```

```python
import jax
import jax.numpy as jnp
from jax import lax
from jax.experimental import pallas as pl
from jax.experimental.layout import Layout, with_layout_constraint
from jax.experimental.pallas import tpu as pltpu
from jax.sharding import Mesh, PartitionSpec as P

HEAD = 128
ROW = ("zlo", "y")
COL = ("zhi", "x", "core")
NZLO, NY, NZHI, NX, NCORE = 3, 8, 4, 4, 2
SLAB = HEAD // NY
F32 = jnp.float32
BF = jnp.bfloat16
SMEM = pl.BlockSpec(memory_space=pltpu.SMEM)
VMEM = pl.BlockSpec(memory_space=pltpu.VMEM)
HBM = pl.BlockSpec(memory_space=pltpu.HBM)


def scene_of(lengths, count):
    ends = jnp.cumsum(lengths)
    places = jnp.arange(count)
    return jnp.sum((places[:, None] >= ends[None, :]).astype(jnp.int32), axis=1)


def lookup(ids, table):
    picks = (ids[:, None] == jnp.arange(table.shape[0])[None, :]).astype(table.dtype)
    return jnp.dot(picks, table, preferred_element_type=F32)


def dot(a, b, dims):
    return lax.dot_general(a, b, (dims, ((), ())), preferred_element_type=F32)


def shift(value, axis, size, step):
    return lax.ppermute(value, axis, [(i, (i + step) % size) for i in range(size)])


def gather_x(value):
    return lax.all_to_all(value, "x", split_axis=0, concat_axis=0, tiled=True)


def after(value, *others):
    return lax.optimization_barrier((value,) + others)[0]


def call(body, out_shape, in_specs, out_specs, flops, nbytes, scratch=(), limit=60):
    return pl.pallas_call(
        body,
        out_shape=out_shape,
        in_specs=in_specs,
        out_specs=out_specs,
        scratch_shapes=list(scratch),
        compiler_params=pltpu.CompilerParams(vmem_limit_bytes=limit * 1024 * 1024),
        cost_estimate=pl.CostEstimate(flops=flops, bytes_accessed=nbytes, transcendentals=0),
    )


def up_body(place, weight, other, gated, theirs, out):
    core = place[0]
    for x in range(NX):
        for z in range(NZHI):
            head = z * NX + x
            value = dot(weight[head * NCORE + core], gated[...], ((1,), (1,)))
            value = value + dot(other[head], theirs[...], ((1,), (1,)))
            rows = pl.ds((x * NZHI + z) * HEAD, HEAD)
            out[rows, :] = value.astype(BF)


def upstream_part(place, weight, other, gated, theirs):
    toks = gated.shape[0]
    rows = NX * NZHI * HEAD
    return call(
        up_body,
        jax.ShapeDtypeStruct((rows, toks), BF),
        [SMEM] + [VMEM] * 4,
        VMEM,
        4 * rows * toks * gated.shape[1],
        4 * rows * toks,
        limit=16,
    )(place, weight, other, gated, theirs)


def slabs(held, y):
    starts = [h * HEAD + y * SLAB for h in range(held.shape[0] // HEAD)]
    return jnp.concatenate([held[start : start + SLAB, :] for start in starts])


def part_body(held, gated, out_mine, out_theirs, rows):
    toks = held.shape[1]
    for y in range(NY):
        rows[:, y * toks : (y + 1) * toks] = slabs(held, y)
    width = out_mine.shape[1]
    out_theirs[...] = dot(rows[...], gated[:, width:], ((1,), (0,))).astype(BF)
    out_mine[...] = dot(rows[...], gated[:, :width], ((1,), (0,))).astype(BF)


def weight_part(held, gated):
    rows = held.shape[0] // NY
    toks, width = gated.shape
    return call(
        part_body,
        (jax.ShapeDtypeStruct((rows, width // NCORE), BF),) * 2,
        [VMEM] * 2,
        (VMEM, VMEM),
        2 * rows * toks * width,
        2 * rows * toks + 2 * toks * width,
        [pltpu.VMEM((rows, toks), BF)],
        limit=16,
    )(held, gated)


def mix_body(place, weight, other, *refs):
    *pieces, out_mine, out_theirs = refs
    core, x = place[0], place[1]
    held = jnp.concatenate([piece[...] for piece in pieces])
    heads = []
    for i in range(NX):
        chip = lax.rem(x + NX - i, NX)
        heads += [z * NX + chip for z in range(NZHI)]
    theirs = jnp.concatenate([other[head] for head in heads])
    out_theirs[...] = dot(held, theirs, ((0,), (0,))).astype(BF)
    mine = jnp.concatenate([weight[head * NCORE + core] for head in heads])
    out_mine[...] = dot(held, mine, ((0,), (0,)))


def mix_part(place, weight, other, pieces):
    toks, width = pieces[0].shape[1], weight.shape[2]
    rows = sum(p.shape[0] for p in pieces)
    return call(
        mix_body,
        (
            jax.ShapeDtypeStruct((toks, width), F32),
            jax.ShapeDtypeStruct((toks, width), BF),
        ),
        [SMEM] + [VMEM] * (2 + len(pieces)),
        (VMEM, VMEM),
        4 * rows * toks * width,
        2 * rows * (toks + 2 * width),
        limit=16,
    )(place, weight, other, *pieces)


def place_body(place, src, dst, taken, given, in_sems, out_sems):
    core = place[0]
    loads = [pltpu.make_async_copy(src.at[y], taken.at[y], in_sems.at[y]) for y in range(NY)]
    for load in loads:
        load.start()
    for load in loads:
        load.wait()
    stores = []
    for i in range(NX * NCORE * NZHI):
        c, x, z = i // (NX * NZHI), i // NZHI % NX, i % NZHI
        head = (z * NX + x) * NCORE + (core if c == 0 else 1 - core)
        for y in range(NY):
            given[i, y * SLAB : (y + 1) * SLAB, :] = taken[y, i * SLAB : (i + 1) * SLAB, :]
        stores.append(pltpu.make_async_copy(given.at[i], dst.at[head], out_sems.at[i]))
        stores[-1].start()
    for store in stores:
        store.wait()


def put_heads(place, total):
    heads, width = NX * NCORE * NZHI, total.shape[1]
    return call(
        place_body,
        jax.ShapeDtypeStruct((heads, HEAD, width), BF),
        [SMEM, HBM],
        HBM,
        0,
        4 * total.size,
        [
            pltpu.VMEM((NY, heads * SLAB, width), BF),
            pltpu.VMEM((heads, HEAD, width), BF),
            pltpu.SemaphoreType.DMA((NY,)),
            pltpu.SemaphoreType.DMA((heads,)),
        ],
    )(place, total.reshape(NY, heads * SLAB, width)).reshape(total.shape)


def on_device(
    qkv,
    out_weight,
    cotangent,
    scene_lengths,
    bucket_ids,
    sensor_ids,
    gsd_ids,
    step_ids,
    step_table,
    gsd_table,
    sensor_table,
    bucket_table,
):
    toks = qkv.shape[0]
    width = cotangent.shape[1]
    factor = HEAD ** (-0.5)
    core = lax.axis_index("core")
    place = jnp.stack([core, lax.axis_index("x")]).astype(jnp.int32)
    weight = out_weight.reshape(-1, HEAD, width)

    other = weight.reshape(-1, NCORE, HEAD, width)
    other = lax.dynamic_index_in_dim(other, 1 - core, 1, keepdims=False)
    other = shift(other, "core", NCORE, 1)

    segments = scene_of(scene_lengths, toks)
    same = segments[:, None] == segments[None, :]
    queries, keys, values = qkv[:, 0], qkv[:, 1], qkv[:, 2]

    scores = dot(queries, keys, ((1,), (1,))) * factor
    scores = jnp.where(same, scores, -1e30)
    top = jnp.max(scores, axis=-1, keepdims=True)
    weights = jnp.exp(scores - top)
    probs = weights / jnp.sum(weights, axis=-1, keepdims=True)
    rounded = probs.astype(BF)
    attended = dot(values, rounded, ((0,), (1,))).astype(BF)
    attended = with_layout_constraint(attended, Layout((0, 1)))

    ids = (step_ids, gsd_ids, sensor_ids, bucket_ids)
    attended, *ids = lax.optimization_barrier((attended, *ids))
    step_ids, gsd_ids, sensor_ids, bucket_ids = ids
    gate_scene = lookup(step_ids, step_table) + lookup(gsd_ids, gsd_table)
    gate_scene = gate_scene + lookup(sensor_ids, sensor_table) + lookup(bucket_ids, bucket_table)
    member = (segments[:, None] == jnp.arange(scene_lengths.shape[0])[None, :]).astype(F32)
    gate = jnp.dot(member, gate_scene, precision=lax.Precision.HIGHEST, preferred_element_type=F32)
    gated = (gate * cotangent.astype(F32)).astype(BF)

    attended, gated = lax.optimization_barrier((attended, gated))
    theirs = shift(gated, "core", NCORE, 1)
    both = jnp.concatenate([gated, theirs], axis=1)
    gated_y = lax.all_gather(both, "y", axis=0, tiled=True)
    natural = attended
    attended = lax.all_to_all(attended, "y", split_axis=0, concat_axis=0, tiled=True)

    summed = upstream_part(place, weight, other, gated, theirs)
    attended, summed = lax.optimization_barrier((attended, summed))
    summed = lax.psum_scatter(summed, "x", scatter_dimension=0, tiled=True)

    own = lax.all_gather(attended, "zhi", axis=0, tiled=True)
    natural = after(natural, own)
    own = gather_x(jnp.concatenate([own] * NX))

    whole = lax.all_gather(natural, "zhi", axis=0, tiled=True)
    own, whole = lax.optimization_barrier((own, whole))

    total, swap = weight_part(own, gated_y)
    total = jnp.concatenate([total, shift(swap, "core", NCORE, 1)])
    total = lax.all_gather(total, "zlo").astype(F32).sum(0).astype(BF)
    whole = after(whole, total)
    summed = after(summed, total)
    total = lax.all_gather(total, "y", axis=0, tiled=True)
    total = put_heads(place, total)

    summed = lax.all_to_all(summed, "zhi", split_axis=0, concat_axis=0, tiled=True)
    summed = summed.reshape(NZHI, HEAD, toks).astype(F32).sum(0).astype(BF)

    whole = [whole] + [shift(whole, "x", NX, i) for i in (1, 2, 3)]

    upstream = summed.T
    grad_values = dot(rounded, upstream, ((0,), (0,))).astype(BF)
    grad_probs = dot(upstream, values, ((1,), (1,)))
    inner = jnp.sum(probs * grad_probs, axis=-1, keepdims=True)
    grad_scores = (probs * (grad_probs - inner)).astype(BF)
    grad_queries = (dot(grad_scores, keys, ((1,), (0,))) * factor).astype(BF)
    grad_keys = (dot(grad_scores, queries, ((0,), (0,))) * factor).astype(BF)
    grad_qkv = jnp.stack([grad_queries, grad_keys, grad_values], axis=1)

    *whole, grad_qkv = lax.optimization_barrier((*whole, grad_qkv))
    mixed, swap = mix_part(place, weight, other, whole)
    mixed = (gate * (mixed + shift(swap, "core", NCORE, 1).astype(F32))).astype(BF)
    return (mixed, grad_qkv, total)


def solution(mesh):
    fine = Mesh(mesh.devices.reshape(NZLO, NY, NZHI, NX, NCORE), ROW + COL)
    return jax.shard_map(
        on_device,
        mesh=fine,
        in_specs=(
            P(ROW, None, COL),
            P(None, COL),
            P(ROW, COL),
            P(ROW),
            P(ROW),
            P(ROW),
            P(ROW),
            P(ROW),
            P(None, COL),
            P(None, COL),
            P(None, COL),
            P(None, COL),
        ),
        out_specs=(P(ROW, COL), P(ROW, None, COL), P(None, COL)),
        check_vma=False,
    )
```

```python
import jax
import jax.numpy as jnp
from jax import lax
from jax.experimental import pallas as pl
from jax.experimental.layout import Layout, with_layout_constraint
from jax.experimental.pallas import tpu as pltpu
from jax.sharding import Mesh, PartitionSpec as P

HEAD = 128
ROW = ("zlo", "y")
COL = ("zhi", "x", "core")
NZLO, NY, NZHI, NX, NCORE = 3, 8, 4, 4, 2
SLAB = HEAD // NY
F32 = jnp.float32
BF = jnp.bfloat16
SMEM = pl.BlockSpec(memory_space=pltpu.SMEM)
VMEM = pl.BlockSpec(memory_space=pltpu.VMEM)
HBM = pl.BlockSpec(memory_space=pltpu.HBM)


def scene_of(lengths, count):
    ends = jnp.cumsum(lengths)
    places = jnp.arange(count)
    return jnp.sum((places[:, None] >= ends[None, :]).astype(jnp.int32), axis=1)


def lookup(ids, table):
    picks = (ids[:, None] == jnp.arange(table.shape[0])[None, :]).astype(table.dtype)
    return jnp.dot(picks, table, preferred_element_type=F32)


def dot(a, b, dims):
    return lax.dot_general(a, b, (dims, ((), ())), preferred_element_type=F32)


def shift(value, axis, size, step):
    return lax.ppermute(value, axis, [(i, (i + step) % size) for i in range(size)])


def gather_x(value):
    return lax.all_to_all(value, "x", split_axis=0, concat_axis=0, tiled=True)


def after(value, *others):
    return lax.optimization_barrier((value,) + others)[0]


def call(body, out_shape, in_specs, out_specs, flops, nbytes, scratch=(), limit=60):
    return pl.pallas_call(
        body,
        out_shape=out_shape,
        in_specs=in_specs,
        out_specs=out_specs,
        scratch_shapes=list(scratch),
        compiler_params=pltpu.CompilerParams(vmem_limit_bytes=limit * 1024 * 1024),
        cost_estimate=pl.CostEstimate(flops=flops, bytes_accessed=nbytes, transcendentals=0),
    )


def up_body(place, weight, other, gated, theirs, out):
    core = place[0]
    for x in range(NX):
        for z in range(NZHI):
            head = z * NX + x
            value = dot(weight[head * NCORE + core], gated[...], ((1,), (1,)))
            value = value + dot(other[head], theirs[...], ((1,), (1,)))
            rows = pl.ds((x * NZHI + z) * HEAD, HEAD)
            out[rows, :] = value.astype(BF)


def upstream_part(place, weight, other, gated, theirs):
    toks = gated.shape[0]
    rows = NX * NZHI * HEAD
    return call(
        up_body,
        jax.ShapeDtypeStruct((rows, toks), BF),
        [SMEM] + [VMEM] * 4,
        VMEM,
        4 * rows * toks * gated.shape[1],
        4 * rows * toks,
        limit=16,
    )(place, weight, other, gated, theirs)


def slabs(held, y):
    starts = [h * HEAD + y * SLAB for h in range(held.shape[0] // HEAD)]
    return jnp.concatenate([held[start : start + SLAB, :] for start in starts])


def part_body(held, gated, out_mine, out_theirs, rows):
    toks = held.shape[1]
    for y in range(NY):
        rows[:, y * toks : (y + 1) * toks] = slabs(held, y)
    width = out_mine.shape[1]
    out_theirs[...] = dot(rows[...], gated[:, width:], ((1,), (0,))).astype(BF)
    out_mine[...] = dot(rows[...], gated[:, :width], ((1,), (0,))).astype(BF)


def weight_part(held, gated):
    rows = held.shape[0] // NY
    toks, width = gated.shape
    return call(
        part_body,
        (jax.ShapeDtypeStruct((rows, width // NCORE), BF),) * 2,
        [VMEM] * 2,
        (VMEM, VMEM),
        2 * rows * toks * width,
        2 * rows * toks + 2 * toks * width,
        [pltpu.VMEM((rows, toks), BF)],
        limit=16,
    )(held, gated)


def mix_body(place, weight, other, *refs):
    *pieces, out_mine, out_theirs = refs
    core, x = place[0], place[1]
    held = jnp.concatenate([piece[...] for piece in pieces])
    heads = []
    for i in range(NX):
        chip = lax.rem(x + NX - i, NX)
        heads += [z * NX + chip for z in range(NZHI)]
    theirs = jnp.concatenate([other[head] for head in heads])
    out_theirs[...] = dot(held, theirs, ((0,), (0,))).astype(BF)
    mine = jnp.concatenate([weight[head * NCORE + core] for head in heads])
    out_mine[...] = dot(held, mine, ((0,), (0,)))


def mix_part(place, weight, other, pieces):
    toks, width = pieces[0].shape[1], weight.shape[2]
    rows = sum(p.shape[0] for p in pieces)
    return call(
        mix_body,
        (
            jax.ShapeDtypeStruct((toks, width), F32),
            jax.ShapeDtypeStruct((toks, width), BF),
        ),
        [SMEM] + [VMEM] * (2 + len(pieces)),
        (VMEM, VMEM),
        4 * rows * toks * width,
        2 * rows * (toks + 2 * width),
        limit=16,
    )(place, weight, other, *pieces)


def place_body(place, src, dst, taken, given, in_sems, out_sems):
    core = place[0]
    loads = [pltpu.make_async_copy(src.at[y], taken.at[y], in_sems.at[y]) for y in range(NY)]
    for load in loads:
        load.start()
    for y in range(NY):
        loads[y].wait()
        for i in range(NX * NCORE * NZHI):
            given[i, y * SLAB : (y + 1) * SLAB, :] = taken[y, i * SLAB : (i + 1) * SLAB, :]
    stores = []
    for i in range(NX * NCORE * NZHI):
        c, x, z = i // (NX * NZHI), i // NZHI % NX, i % NZHI
        head = (z * NX + x) * NCORE + (core if c == 0 else 1 - core)
        stores.append(pltpu.make_async_copy(given.at[i], dst.at[head], out_sems.at[i]))
        stores[-1].start()
    for store in stores:
        store.wait()


def put_heads(place, total):
    heads, width = NX * NCORE * NZHI, total.shape[1]
    return call(
        place_body,
        jax.ShapeDtypeStruct((heads, HEAD, width), BF),
        [SMEM, HBM],
        HBM,
        0,
        4 * total.size,
        [
            pltpu.VMEM((NY, heads * SLAB, width), BF),
            pltpu.VMEM((heads, HEAD, width), BF),
            pltpu.SemaphoreType.DMA((NY,)),
            pltpu.SemaphoreType.DMA((heads,)),
        ],
    )(place, total.reshape(NY, heads * SLAB, width)).reshape(total.shape)


def on_device(
    qkv,
    out_weight,
    cotangent,
    scene_lengths,
    bucket_ids,
    sensor_ids,
    gsd_ids,
    step_ids,
    step_table,
    gsd_table,
    sensor_table,
    bucket_table,
):
    toks = qkv.shape[0]
    width = cotangent.shape[1]
    factor = HEAD ** (-0.5)
    core = lax.axis_index("core")
    place = jnp.stack([core, lax.axis_index("x")]).astype(jnp.int32)
    weight = out_weight.reshape(-1, HEAD, width)

    other = weight.reshape(-1, NCORE, HEAD, width)
    other = lax.dynamic_index_in_dim(other, 1 - core, 1, keepdims=False)
    other = shift(other, "core", NCORE, 1)

    segments = scene_of(scene_lengths, toks)
    same = segments[:, None] == segments[None, :]
    queries, keys, values = qkv[:, 0], qkv[:, 1], qkv[:, 2]

    scores = dot(queries, keys, ((1,), (1,))) * factor
    scores = jnp.where(same, scores, -1e30)
    top = jnp.max(scores, axis=-1, keepdims=True)
    weights = jnp.exp(scores - top)
    probs = weights / jnp.sum(weights, axis=-1, keepdims=True)
    rounded = probs.astype(BF)
    attended = dot(values, rounded, ((0,), (1,))).astype(BF)
    attended = with_layout_constraint(attended, Layout((0, 1)))

    ids = (step_ids, gsd_ids, sensor_ids, bucket_ids)
    attended, *ids = lax.optimization_barrier((attended, *ids))
    step_ids, gsd_ids, sensor_ids, bucket_ids = ids
    gate_scene = lookup(step_ids, step_table) + lookup(gsd_ids, gsd_table)
    gate_scene = gate_scene + lookup(sensor_ids, sensor_table) + lookup(bucket_ids, bucket_table)
    member = (segments[:, None] == jnp.arange(scene_lengths.shape[0])[None, :]).astype(F32)
    gate = jnp.dot(member, gate_scene, precision=lax.Precision.HIGHEST, preferred_element_type=F32)
    gated = (gate * cotangent.astype(F32)).astype(BF)

    attended, gated = lax.optimization_barrier((attended, gated))
    theirs = shift(gated, "core", NCORE, 1)
    both = jnp.concatenate([gated, theirs], axis=1)
    gated_y = lax.all_gather(both, "y", axis=0, tiled=True)
    natural = attended
    attended = lax.all_to_all(attended, "y", split_axis=0, concat_axis=0, tiled=True)

    summed = upstream_part(place, weight, other, gated, theirs)
    attended, summed = lax.optimization_barrier((attended, summed))
    summed = lax.psum_scatter(summed, "x", scatter_dimension=0, tiled=True)

    own = lax.all_gather(attended, "zhi", axis=0, tiled=True)
    natural = after(natural, own)
    own = gather_x(jnp.concatenate([own] * NX))

    whole = lax.all_gather(natural, "zhi", axis=0, tiled=True)
    own, whole = lax.optimization_barrier((own, whole))

    total, swap = weight_part(own, gated_y)
    total = jnp.concatenate([total, shift(swap, "core", NCORE, 1)])
    rows = total.shape[0]
    total = lax.all_gather(total, "zlo", axis=0, tiled=True)
    terms = [total[i * rows : (i + 1) * rows].astype(F32) for i in range(NZLO)]
    total = (terms[0] + terms[1] + terms[2]).astype(BF)
    whole = after(whole, total)
    summed = after(summed, total)
    total = lax.all_gather(total, "y", axis=0, tiled=True)
    total = put_heads(place, total)

    summed = lax.all_to_all(summed, "zhi", split_axis=0, concat_axis=0, tiled=True)
    summed = summed.reshape(NZHI, HEAD, toks).astype(F32).sum(0).astype(BF)

    whole = [whole] + [shift(whole, "x", NX, i) for i in (1, 2, 3)]

    upstream = summed.T
    grad_values = dot(rounded, upstream, ((0,), (0,))).astype(BF)
    grad_probs = dot(upstream, values, ((1,), (1,)))
    inner = jnp.sum(probs * grad_probs, axis=-1, keepdims=True)
    grad_scores = (probs * (grad_probs - inner)).astype(BF)
    grad_queries = (dot(grad_scores, keys, ((1,), (0,))) * factor).astype(BF)
    grad_keys = (dot(grad_scores, queries, ((0,), (0,))) * factor).astype(BF)
    grad_qkv = jnp.stack([grad_queries, grad_keys, grad_values], axis=1)

    *whole, grad_qkv = lax.optimization_barrier((*whole, grad_qkv))
    mixed, swap = mix_part(place, weight, other, whole)
    mixed = (gate * (mixed + shift(swap, "core", NCORE, 1).astype(F32))).astype(BF)
    return (mixed, grad_qkv, total)


def solution(mesh):
    fine = Mesh(mesh.devices.reshape(NZLO, NY, NZHI, NX, NCORE), ROW + COL)
    return jax.shard_map(
        on_device,
        mesh=fine,
        in_specs=(
            P(ROW, None, COL),
            P(None, COL),
            P(ROW, COL),
            P(ROW),
            P(ROW),
            P(ROW),
            P(ROW),
            P(ROW),
            P(None, COL),
            P(None, COL),
            P(None, COL),
            P(None, COL),
        ),
        out_specs=(P(ROW, COL), P(ROW, None, COL), P(None, COL)),
        check_vma=False,
    )
```

```python
import jax
import jax.numpy as jnp
from jax import lax
from jax.experimental import pallas as pl
from jax.experimental.layout import Layout, with_layout_constraint
from jax.experimental.pallas import tpu as pltpu
from jax.sharding import Mesh, PartitionSpec as P

HEAD = 128
ROW = ("zlo", "y")
COL = ("zhi", "x", "core")
NZLO, NY, NZHI, NX, NCORE = 3, 8, 4, 4, 2
SLAB = HEAD // NY
F32 = jnp.float32
BF = jnp.bfloat16
SMEM = pl.BlockSpec(memory_space=pltpu.SMEM)
VMEM = pl.BlockSpec(memory_space=pltpu.VMEM)
HBM = pl.BlockSpec(memory_space=pltpu.HBM)


def scene_of(lengths, count):
    ends = jnp.cumsum(lengths)
    places = jnp.arange(count)
    return jnp.sum((places[:, None] >= ends[None, :]).astype(jnp.int32), axis=1)


def lookup(ids, table):
    picks = (ids[:, None] == jnp.arange(table.shape[0])[None, :]).astype(table.dtype)
    return jnp.dot(picks, table, preferred_element_type=F32)


def dot(a, b, dims):
    return lax.dot_general(a, b, (dims, ((), ())), preferred_element_type=F32)


def shift(value, axis, size, step):
    return lax.ppermute(value, axis, [(i, (i + step) % size) for i in range(size)])


def gather_x(value):
    return lax.all_to_all(value, "x", split_axis=0, concat_axis=0, tiled=True)


def after(value, *others):
    return lax.optimization_barrier((value,) + others)[0]


def call(body, out_shape, in_specs, out_specs, flops, nbytes, scratch=(), limit=60):
    return pl.pallas_call(
        body,
        out_shape=out_shape,
        in_specs=in_specs,
        out_specs=out_specs,
        scratch_shapes=list(scratch),
        compiler_params=pltpu.CompilerParams(vmem_limit_bytes=limit * 1024 * 1024),
        cost_estimate=pl.CostEstimate(flops=flops, bytes_accessed=nbytes, transcendentals=0),
    )


def up_body(place, weight, other, gated, theirs, out):
    core = place[0]
    for x in range(NX):
        for z in range(NZHI):
            head = z * NX + x
            value = dot(weight[head * NCORE + core], gated[...], ((1,), (1,)))
            value = value + dot(other[head], theirs[...], ((1,), (1,)))
            rows = pl.ds((x * NZHI + z) * HEAD, HEAD)
            out[rows, :] = value.astype(BF)


def upstream_part(place, weight, other, gated, theirs):
    toks = gated.shape[0]
    rows = NX * NZHI * HEAD
    return call(
        up_body,
        jax.ShapeDtypeStruct((rows, toks), BF),
        [SMEM] + [VMEM] * 4,
        VMEM,
        4 * rows * toks * gated.shape[1],
        4 * rows * toks,
        limit=16,
    )(place, weight, other, gated, theirs)


def slabs(held, y):
    starts = [h * HEAD + y * SLAB for h in range(held.shape[0] // HEAD)]
    return jnp.concatenate([held[start : start + SLAB, :] for start in starts])


def part_body(held, gated, out_mine, out_theirs, rows):
    toks = held.shape[1]
    for y in range(NY):
        rows[:, y * toks : (y + 1) * toks] = slabs(held, y)
    width = out_mine.shape[1]
    out_theirs[...] = dot(rows[...], gated[:, width:], ((1,), (0,))).astype(BF)
    out_mine[...] = dot(rows[...], gated[:, :width], ((1,), (0,))).astype(BF)


def weight_part(held, gated):
    rows = held.shape[0] // NY
    toks, width = gated.shape
    return call(
        part_body,
        (jax.ShapeDtypeStruct((rows, width // NCORE), BF),) * 2,
        [VMEM] * 2,
        (VMEM, VMEM),
        2 * rows * toks * width,
        2 * rows * toks + 2 * toks * width,
        [pltpu.VMEM((rows, toks), BF)],
        limit=16,
    )(held, gated)


def mix_body(place, weight, other, *refs):
    *pieces, out_mine, out_theirs = refs
    core, x = place[0], place[1]
    held = jnp.concatenate([piece[...] for piece in pieces])
    heads = []
    for i in range(NX):
        chip = lax.rem(x + NX - i, NX)
        heads += [z * NX + chip for z in range(NZHI)]
    theirs = jnp.concatenate([other[head] for head in heads])
    out_theirs[...] = dot(held, theirs, ((0,), (0,))).astype(BF)
    mine = jnp.concatenate([weight[head * NCORE + core] for head in heads])
    out_mine[...] = dot(held, mine, ((0,), (0,)))


def mix_part(place, weight, other, pieces):
    toks, width = pieces[0].shape[1], weight.shape[2]
    rows = sum(p.shape[0] for p in pieces)
    return call(
        mix_body,
        (
            jax.ShapeDtypeStruct((toks, width), F32),
            jax.ShapeDtypeStruct((toks, width), BF),
        ),
        [SMEM] + [VMEM] * (2 + len(pieces)),
        (VMEM, VMEM),
        4 * rows * toks * width,
        2 * rows * (toks + 2 * width),
        limit=16,
    )(place, weight, other, *pieces)


def place_body(place, src, dst, taken, given, in_sems, out_sems):
    core = place[0]
    loads = [pltpu.make_async_copy(src.at[y], taken.at[y], in_sems.at[y]) for y in range(NY)]
    for load in loads:
        load.start()
    for y in range(NY):
        loads[y].wait()
        for i in range(NX * NCORE * NZHI):
            given[i, y * SLAB : (y + 1) * SLAB, :] = taken[y, i * SLAB : (i + 1) * SLAB, :]
    stores = []
    for i in range(NX * NCORE * NZHI):
        c, x, z = i // (NX * NZHI), i // NZHI % NX, i % NZHI
        head = (z * NX + x) * NCORE + (core if c == 0 else 1 - core)
        stores.append(pltpu.make_async_copy(given.at[i], dst.at[head], out_sems.at[i]))
        stores[-1].start()
    for store in stores:
        store.wait()


def put_heads(place, total):
    heads, width = NX * NCORE * NZHI, total.shape[1]
    return call(
        place_body,
        jax.ShapeDtypeStruct((heads, HEAD, width), BF),
        [SMEM, HBM],
        HBM,
        0,
        4 * total.size,
        [
            pltpu.VMEM((NY, heads * SLAB, width), BF),
            pltpu.VMEM((heads, HEAD, width), BF),
            pltpu.SemaphoreType.DMA((NY,)),
            pltpu.SemaphoreType.DMA((heads,)),
        ],
    )(place, total.reshape(NY, heads * SLAB, width)).reshape(total.shape)


def on_device(
    qkv,
    out_weight,
    cotangent,
    scene_lengths,
    bucket_ids,
    sensor_ids,
    gsd_ids,
    step_ids,
    step_table,
    gsd_table,
    sensor_table,
    bucket_table,
):
    toks = qkv.shape[0]
    width = cotangent.shape[1]
    factor = HEAD ** (-0.5)
    core = lax.axis_index("core")
    place = jnp.stack([core, lax.axis_index("x")]).astype(jnp.int32)
    weight = out_weight.reshape(-1, HEAD, width)

    other = weight.reshape(-1, NCORE, HEAD, width)
    other = lax.dynamic_index_in_dim(other, 1 - core, 1, keepdims=False)
    other = shift(other, "core", NCORE, 1)

    segments = scene_of(scene_lengths, toks)
    same = segments[:, None] == segments[None, :]
    queries, keys, values = qkv[:, 0], qkv[:, 1], qkv[:, 2]

    scores = dot(queries, keys, ((1,), (1,))) * factor
    scores = jnp.where(same, scores, -1e30)
    top = jnp.max(scores, axis=-1, keepdims=True)
    weights = jnp.exp(scores - top)
    probs = weights / jnp.sum(weights, axis=-1, keepdims=True)
    rounded = probs.astype(BF)
    attended = dot(values, rounded, ((0,), (1,))).astype(BF)
    attended = with_layout_constraint(attended, Layout((0, 1)))

    ids = (step_ids, gsd_ids, sensor_ids, bucket_ids)
    attended, *ids = lax.optimization_barrier((attended, *ids))
    step_ids, gsd_ids, sensor_ids, bucket_ids = ids
    gate_scene = lookup(step_ids, step_table) + lookup(gsd_ids, gsd_table)
    gate_scene = gate_scene + lookup(sensor_ids, sensor_table) + lookup(bucket_ids, bucket_table)
    member = (segments[:, None] == jnp.arange(scene_lengths.shape[0])[None, :]).astype(F32)
    gate = jnp.dot(member, gate_scene, precision=lax.Precision.HIGHEST, preferred_element_type=F32)
    gated = (gate * cotangent.astype(F32)).astype(BF)

    attended, gated = lax.optimization_barrier((attended, gated))
    theirs = shift(gated, "core", NCORE, 1)
    both = jnp.concatenate([gated, theirs], axis=1)
    natural = attended
    attended = lax.all_to_all(attended, "y", split_axis=0, concat_axis=0, tiled=True)

    summed = upstream_part(place, weight, other, gated, theirs)
    attended, summed, both = lax.optimization_barrier((attended, summed, both))
    gated_y = lax.all_gather(both, "y", axis=0, tiled=True)
    summed = lax.psum_scatter(summed, "x", scatter_dimension=0, tiled=True)

    own = lax.all_gather(attended, "zhi", axis=0, tiled=True)
    natural = after(natural, own)
    own = gather_x(jnp.concatenate([own] * NX))

    whole = lax.all_gather(natural, "zhi", axis=0, tiled=True)
    own, whole = lax.optimization_barrier((own, whole))

    total, swap = weight_part(own, gated_y)
    total = jnp.concatenate([total, shift(swap, "core", NCORE, 1)])
    rows = total.shape[0]
    total = lax.all_gather(total, "zlo", axis=0, tiled=True)
    terms = [total[i * rows : (i + 1) * rows].astype(F32) for i in range(NZLO)]
    total = (terms[0] + terms[1] + terms[2]).astype(BF)
    whole = after(whole, total)
    summed = after(summed, total)
    total = lax.all_gather(total, "y", axis=0, tiled=True)
    total = put_heads(place, total)

    summed = lax.all_to_all(summed, "zhi", split_axis=0, concat_axis=0, tiled=True)
    summed = summed.reshape(NZHI, HEAD, toks).astype(F32).sum(0).astype(BF)

    whole = [whole] + [shift(whole, "x", NX, i) for i in (1, 2, 3)]

    upstream = summed.T
    grad_values = dot(rounded, upstream, ((0,), (0,))).astype(BF)
    grad_probs = dot(upstream, values, ((1,), (1,)))
    inner = jnp.sum(probs * grad_probs, axis=-1, keepdims=True)
    grad_scores = (probs * (grad_probs - inner)).astype(BF)
    grad_queries = (dot(grad_scores, keys, ((1,), (0,))) * factor).astype(BF)
    grad_keys = (dot(grad_scores, queries, ((0,), (0,))) * factor).astype(BF)
    grad_qkv = jnp.stack([grad_queries, grad_keys, grad_values], axis=1)

    *whole, grad_qkv = lax.optimization_barrier((*whole, grad_qkv))
    mixed, swap = mix_part(place, weight, other, whole)
    mixed = (gate * (mixed + shift(swap, "core", NCORE, 1).astype(F32))).astype(BF)
    return (mixed, grad_qkv, total)


def solution(mesh):
    fine = Mesh(mesh.devices.reshape(NZLO, NY, NZHI, NX, NCORE), ROW + COL)
    return jax.shard_map(
        on_device,
        mesh=fine,
        in_specs=(
            P(ROW, None, COL),
            P(None, COL),
            P(ROW, COL),
            P(ROW),
            P(ROW),
            P(ROW),
            P(ROW),
            P(ROW),
            P(None, COL),
            P(None, COL),
            P(None, COL),
            P(None, COL),
        ),
        out_specs=(P(ROW, COL), P(ROW, None, COL), P(None, COL)),
        check_vma=False,
    )
```
